256 devices in a mesh: dp: 8 (over z_lo, y), seq: 32 (over x, z_hi, core).
Axes of the slice: x: 4, y: 4, z: 8 (z_hi: 4, z_lo: 2; z = z_hi * 2 + z_lo), core: 2. Of those that a mesh axis runs over, the one named last changes fastest.
Arguments:
- tokens: bfloat16 [8, 8192, 4096], P('dp', 'seq'), may hold values from -6 to 6
- queries: bfloat16 [8, 8192, 128], P('dp', 'seq'), may hold values from -6 to 6
- key_vectors: bfloat16 [8, 8192, 128], P('dp', 'seq'), may hold values from -6 to 6
- doc_position: int32 [8, 8192], P('dp', 'seq'), may hold values from 0 to 8191, as said below
- value_scores: float32 [8, 8192, 4], P('dp', 'seq'), may hold values from 0.1 to 1
- value_experts: int32 [8, 8192, 2], P('dp', 'seq'), may hold values from 0 to 3, all different within a row
- output_scores: float32 [8, 8192, 4], P('dp', 'seq'), may hold values from 0.1 to 1
- output_experts: int32 [8, 8192, 2], P('dp', 'seq'), may hold values from 0 to 3, all different within a row
- value_panels: bfloat16 [4096, 512], P('seq'), may hold values from -0.09375 to 0.09375
- output_panels: bfloat16 [4096, 512], P('seq'), may hold values from -3 to 3
- cotangent: bfloat16 [8, 8192, 4096], P('dp', 'seq'), may hold values from -0.625 to 0.625
Outputs:
- layer_output: bfloat16 [8, 8192, 4096], P('dp', 'seq')
- grad_tokens: bfloat16 [8, 8192, 4096], P('dp', 'seq')
- grad_queries: bfloat16 [8, 8192, 128], P('dp', 'seq')
- grad_keys: bfloat16 [8, 8192, 128], P('dp', 'seq')
- grad_value: float32 [4096, 512], P('seq')
- grad_output: float32 [4096, 512], P('seq')
The draws below stay inside these ranges and needn't reach their ends.
Inputs may be any that keep to these rules, and one draw needn't show every extreme that they name: doc_position[b, i] is i minus the first position of the document that holds position i; position 0 starts a document in every sequence; sequence 0 is one document; every other sequence holds one to four documents.
All inputs are finite; a program needn't handle non-finite values.
Results may differ from the reference program's by a relative error of at most 0.035.
Values may be sent and summed in bfloat16 or wider, within the bound.
No kernel may reach another device: no remote copies, remote signals or barrier semaphores. Data moves between devices by JAX's collectives and lax.ppermute only.
A program may use at most 128 MiB of HBM per device.

```python
import math
import jax
import jax.numpy as jnp
from jax import lax

D = 4096
DH = 128
EXPERTS = 4
TOPK = 2
TOK_DEV = 256
LENGTH = 8192
BATCH = 8
N_SEQ = 32


def joint_draw(key):
    folded = jax.random.fold_in(key, 17)
    streams = jax.random.split(folded, 2)
    full_shape = (BATCH, LENGTH, DH)
    query_vals = jnp.clip(1.4 * jax.random.normal(streams[0], full_shape, jnp.float32), -6.0, 6.0)
    key_vals = jnp.clip(1.4 * jax.random.normal(streams[1], full_shape, jnp.float32), -6.0, 6.0)
    return (query_vals, key_vals)


def draw_queries(key, part):
    return joint_draw(key)[0].astype(jnp.bfloat16)


def draw_key_vectors(key, part):
    return joint_draw(key)[1].astype(jnp.bfloat16)


def draw_doc_position(key, part):
    boundaries = jax.random.randint(jax.random.fold_in(key, 5), (BATCH, 3), 1, LENGTH)
    positions = jnp.arange(LENGTH, dtype=jnp.int32)
    starts_doc = jnp.any(positions[None, :, None] == boundaries[:, None, :], axis=2)
    starts_doc = starts_doc & (jnp.arange(BATCH, dtype=jnp.int32)[:, None] > 0)
    starts_doc = starts_doc | (positions[None, :] == 0)
    start_marks = jnp.where(starts_doc, positions[None, :], 0)
    last_start = lax.cummax(start_marks, axis=1)
    return (positions[None, :] - last_start).astype(jnp.int32)


def spiked(values, own_key, source, target, blocks, factor):
    owner, partner = [(jnp.arange(values.shape[axis_at]) // (values.shape[axis_at] // blocks)).reshape([-1 if axis == axis_at else 1 for axis in range(values.ndim)]) for axis_at in (source, target)]
    chosen = jax.random.permutation(own_key, blocks)[partner]
    strong = (owner == chosen) | (owner == (partner + blocks // 2) % blocks)
    return jnp.where(strong, factor * values, values)


def level_of(stream_key, shape, cuts, low, top_value):
    factor_of, own = 1.0, jax.random.fold_in(stream_key, 6)
    for position, parts in cuts:
        heights = jnp.exp(jax.random.uniform(jax.random.fold_in(own, position), (parts,), jnp.float32, low / len(cuts), top_value / len(cuts)))
        factor_of = factor_of * jnp.repeat(heights, shape[position] // parts).reshape([-1 if axis == position else 1 for axis in range(len(shape))])
    return factor_of


def different_ones(own_key, rows, amount, top, lift):
    ranking = jax.random.permutation(jax.random.fold_in(own_key, 1), amount)
    boost = ranking
    for power in range(3):
        boost = boost * boost // amount
    boost = boost * lift // amount
    lots = jax.random.randint(jax.random.fold_in(own_key, 2), (rows, amount), 0, 4096) + boost
    holders = jax.random.permutation(jax.random.fold_in(own_key, 3), rows)[jnp.arange(amount) % rows]
    lots = jnp.where(jnp.arange(rows)[:, None] == holders[None, :], 1 << 14, lots)
    merit = lots * amount + jnp.arange(amount)
    return lax.top_k(merit.astype(jnp.int32), top)[1].astype(jnp.int32)


def centred(key, extent, scale, bound, pieces=(), kind=jnp.bfloat16):
    drawn = scale * jax.random.normal(key, extent, jnp.float32)
    if pieces:
        drawn = drawn * level_of(key, extent, pieces, -0.22, 0.18)
    return jnp.clip(drawn, -bound, bound).astype(kind)


def noise_with(stream_key, shape, scale, reach, cuts, heavy, kind=jnp.bfloat16):
    result = scale * jax.random.normal(stream_key, shape, jnp.float32)
    if cuts:
        result = result * level_of(stream_key, shape, cuts, -0.22, 0.18)
    return jnp.clip(spiked(result, jax.random.fold_in(stream_key, 3), *heavy), -reach, reach).astype(kind)


def setup_inputs(seed: int = 0) -> dict:
    key_list = jax.random.split(jax.random.key(seed), 12)
    return {
        "tokens": noise_with(key_list[0], (BATCH, LENGTH, D), 1.0, 6.0, ((0, 8), (1, 32)), (1, 2, 32, 2.75)),
        "queries": draw_queries(jax.random.fold_in(key_list[11], 71), 0),
        "key_vectors": draw_key_vectors(jax.random.fold_in(key_list[11], 71), 0),
        "doc_position": draw_doc_position(jax.random.fold_in(key_list[11], 71), 0),
        "value_scores": jnp.clip(jnp.exp(math.log(1.0) - 2.3025851 * jax.random.uniform(key_list[4], (BATCH, LENGTH, EXPERTS), jnp.float32) ** level_of(key_list[4], (BATCH, LENGTH, EXPERTS), ((0, 8), (1, 32)), -0.2, 0.2)), 0.1, 1.0),
        "value_experts": different_ones(key_list[5], BATCH * LENGTH, EXPERTS, TOPK, 4096).reshape((BATCH, LENGTH, TOPK)),
        "output_scores": jnp.clip(jnp.exp(math.log(1.0) - 2.3025851 * jax.random.uniform(key_list[6], (BATCH, LENGTH, EXPERTS), jnp.float32) ** level_of(key_list[6], (BATCH, LENGTH, EXPERTS), ((0, 8), (1, 32)), -0.2, 0.2)), 0.1, 1.0),
        "output_experts": different_ones(key_list[7], BATCH * LENGTH, EXPERTS, TOPK, 4096).reshape((BATCH, LENGTH, TOPK)),
        "value_panels": centred(key_list[8], (D, EXPERTS * DH), D ** -0.5, 0.09375, ((0, 32),)),
        "output_panels": centred(key_list[9], (D, EXPERTS * DH), 0.5, 3.0, ((0, 32),)),
        "cotangent": noise_with(key_list[10], (BATCH, LENGTH, D), 0.05, 0.625, ((0, 8), (1, 32)), (1, 2, 32, 2.75)),
    }


def expert_gates(scores, chosen):
    chosen_hit = jnp.any(chosen[:, :, None] == jnp.arange(EXPERTS, dtype=jnp.int32)[None, None, :], axis=1)
    return jnp.where(chosen_hit, scores.astype(jnp.float32), jnp.float32(0.0))


def one_sequence(tok_seq, query_seq, key_seq, position_seq, value_scores, value_experts, output_scores, output_experts, value_panels, output_panels, grad_seq):
    value_gate = expert_gates(value_scores, value_experts)
    output_gate = expert_gates(output_scores, output_experts)
    projection = jnp.dot(tok_seq, value_panels, preferred_element_type=jnp.float32)
    value_vec = jnp.sum(projection.reshape(LENGTH, EXPERTS, DH) * value_gate[:, :, None], axis=1).astype(jnp.bfloat16)
    pulled = jnp.dot(grad_seq, output_panels, preferred_element_type=jnp.float32)
    dattended = jnp.sum(pulled.reshape(LENGTH, EXPERTS, DH) * output_gate[:, :, None], axis=1).astype(jnp.bfloat16)
    block_rows = math.gcd(LENGTH, 512)
    block_count = LENGTH // block_rows
    key_index = jnp.arange(LENGTH, dtype=jnp.int32)
    score_scale = DH ** -0.5

    def attend_block(carried, offset):
        dkey_sum, dvalue_sum = carried
        query_block = lax.dynamic_slice_in_dim(query_seq, offset, block_rows, 0)
        limit_block = lax.dynamic_slice_in_dim(position_seq, offset, block_rows, 0)
        dattended_block = lax.dynamic_slice_in_dim(dattended, offset, block_rows, 0)
        query_index = offset + jnp.arange(block_rows, dtype=jnp.int32)
        visible = (key_index[None, :] <= query_index[:, None]) & (query_index[:, None] - key_index[None, :] <= limit_block[:, None])
        scores = jnp.dot(query_block, key_seq.T, preferred_element_type=jnp.float32) * score_scale
        masked = jnp.where(visible, scores, -jnp.inf)
        row_max = jnp.max(masked, axis=1)
        log_total = row_max + jnp.log(jnp.sum(jnp.exp(masked - row_max[:, None]), axis=1))
        attn_prob = jnp.exp(masked - log_total[:, None])
        prob_low = attn_prob.astype(jnp.bfloat16)
        attended = jnp.dot(prob_low, value_vec, preferred_element_type=jnp.float32).astype(jnp.bfloat16)
        row_delta = jnp.sum(dattended_block.astype(jnp.float32) * attended.astype(jnp.float32), axis=1)
        dweights = jnp.dot(dattended_block, value_vec.T, preferred_element_type=jnp.float32)
        dscores = (attn_prob * (dweights - row_delta[:, None])).astype(jnp.bfloat16)
        grad_query = (jnp.dot(dscores, key_seq, preferred_element_type=jnp.float32) * score_scale).astype(jnp.bfloat16)
        dkey_sum = dkey_sum + jnp.dot(dscores.T, query_block, preferred_element_type=jnp.float32) * score_scale
        dvalue_sum = dvalue_sum + jnp.dot(prob_low.T, dattended_block, preferred_element_type=jnp.float32)
        return (dkey_sum, dvalue_sum), (attended, grad_query)

    offsets = jnp.arange(block_count, dtype=jnp.int32) * block_rows
    zeros_acc = jnp.zeros((LENGTH, DH), jnp.float32)
    (dkey_sum, dvalue_sum), (attended, grad_query) = lax.scan(attend_block, (zeros_acc, zeros_acc), offsets)
    attended = attended.reshape(LENGTH, DH)
    grad_query = grad_query.reshape(LENGTH, DH)
    expanded = (output_gate[:, :, None] * attended.astype(jnp.float32)[:, None, :]).reshape(LENGTH, EXPERTS * DH).astype(jnp.bfloat16)
    layer_output = jnp.dot(expanded, output_panels.T, preferred_element_type=jnp.float32).astype(jnp.bfloat16)
    dvalue = dvalue_sum.astype(jnp.bfloat16)
    value_grad = (value_gate[:, :, None] * dvalue.astype(jnp.float32)[:, None, :]).reshape(LENGTH, EXPERTS * DH).astype(jnp.bfloat16)
    grad_tok = jnp.dot(value_grad, value_panels.T, preferred_element_type=jnp.float32).astype(jnp.bfloat16)

    def weight_block(carried, block_index):
        offset = block_index * TOK_DEV
        tok_slice = lax.dynamic_slice_in_dim(tok_seq, offset, TOK_DEV, 0)
        grad_slice = lax.dynamic_slice_in_dim(grad_seq, offset, TOK_DEV, 0)
        value_slice = lax.dynamic_slice_in_dim(value_grad, offset, TOK_DEV, 0)
        expanded_slice = lax.dynamic_slice_in_dim(expanded, offset, TOK_DEV, 0)
        term_value = jnp.dot(tok_slice.T, value_slice, preferred_element_type=jnp.float32)
        term_output = jnp.dot(grad_slice.T, expanded_slice, preferred_element_type=jnp.float32)
        term_value = lax.optimization_barrier(term_value.astype(jnp.bfloat16)).astype(jnp.float32)
        term_output = lax.optimization_barrier(term_output.astype(jnp.bfloat16)).astype(jnp.float32)
        return (carried[0] + term_value, carried[1] + term_output), None

    weight_zero = jnp.zeros((D, EXPERTS * DH), jnp.float32)
    (grad_value, grad_output), _ = lax.scan(weight_block, (weight_zero, weight_zero), jnp.arange(N_SEQ, dtype=jnp.int32))
    return layer_output, grad_tok, grad_query, dkey_sum.astype(jnp.bfloat16), grad_value, grad_output


def reference(tokens, queries, key_vectors, doc_position, value_scores, value_experts, output_scores, output_experts, value_panels, output_panels, cotangent):
    outputs_list = []
    grad_tok_list = []
    grad_query_list = []
    grad_key_list = []
    grad_value = jnp.zeros((D, EXPERTS * DH), jnp.float32)
    grad_output = jnp.zeros((D, EXPERTS * DH), jnp.float32)
    for seq_index in range(BATCH):
        results = one_sequence(tokens[seq_index], queries[seq_index], key_vectors[seq_index], doc_position[seq_index], value_scores[seq_index], value_experts[seq_index], output_scores[seq_index], output_experts[seq_index], value_panels, output_panels, cotangent[seq_index])
        outputs_list.append(results[0])
        grad_tok_list.append(results[1])
        grad_query_list.append(results[2])
        grad_key_list.append(results[3])
        grad_value = grad_value + results[4]
        grad_output = grad_output + results[5]
    return (jnp.stack(outputs_list), jnp.stack(grad_tok_list), jnp.stack(grad_query_list), jnp.stack(grad_key_list), grad_value, grad_output)
```

```python
import jax
import jax.numpy as jnp
from jax import lax
from jax.sharding import Mesh, PartitionSpec as P

F32 = jnp.float32
BF16 = jnp.bfloat16


def expert_gates(scores, chosen, experts):
    chosen_hit = chosen[:, :, None] == lax.iota(jnp.int32, experts)[None, None, :]
    return jnp.where(jnp.any(chosen_hit, axis=1), scores, F32(0.0))


def contract_last(left, right):
    return lax.dot_general(left, right, (((1,), (1,)), ((), ())), preferred_element_type=F32)


def contract_first(left, right):
    return lax.dot_general(left, right, (((0,), (0,)), ((), ())), preferred_element_type=F32)


def exchange(blocks, axes):
    return lax.all_to_all(blocks, axes, 0, 0, tiled=True)


def share(block, axes, count):
    return exchange(jnp.broadcast_to(block[None], (count,) + block.shape), axes)


def other_core(value):
    return lax.ppermute(value, "c", [(0, 1), (1, 0)])


def body(
    tokens,
    queries,
    key_vectors,
    doc_position,
    value_scores,
    value_experts,
    output_scores,
    output_experts,
    value_panels,
    output_panels,
    cotangent,
):
    n_x, n_y, n_zh, n_zl = 4, 4, 4, 2
    tok_block = tokens[0]
    query_block = queries[0]
    own_keys = key_vectors[0]
    positions = doc_position[0]
    grad_rows = cotangent[0]
    rows, width = tok_block.shape
    head = query_block.shape[1]
    experts = value_scores.shape[2]
    panel_rows, panel_width = value_panels.shape
    half = panel_width // 2
    ix, izh, ic = lax.axis_index("x"), lax.axis_index("zh"), lax.axis_index("c")
    first = ic == 0

    def own_first(pair):
        return jnp.where(first, pair, pair[::-1])

    def gate_own_first(gate):
        return own_first(gate.T.reshape(2, experts // 2, rows)).reshape(experts, rows).T

    value_gate = gate_own_first(expert_gates(value_scores[0], value_experts[0], experts))
    output_gate = expert_gates(output_scores[0], output_experts[0], experts)
    output_gate_own = gate_own_first(output_gate)

    output_full = lax.all_gather(output_panels, ("x", "zh", "c"), axis=0, tiled=True)

    mine = lax.dynamic_slice_in_dim(value_panels, ic * half, half, 1)
    theirs = lax.dynamic_slice_in_dim(value_panels, (1 - ic) * half, half, 1)
    half_rows = own_first(jnp.stack([mine, other_core(theirs)])).reshape(2 * panel_rows, half)
    pos_hi = (positions // 128).astype(BF16)
    pos_lo = (positions % 128).astype(BF16)
    pos_rows = jnp.zeros((16, half + head), BF16)
    pos_rows = pos_rows.at[0, :rows].set(pos_hi).at[1, :rows].set(pos_lo)
    packed = jnp.concatenate(
        [jnp.concatenate([half_rows, query_block], axis=1), pos_rows], axis=0
    )
    packed = share(packed, "zh", n_zh)
    panels_zh = packed[:, :rows, :half].reshape(n_zh * rows, half)
    queries_zh = packed[:, :rows, half:].reshape(n_zh * rows, head)
    pos_zh = packed[:, rows : rows + 2, :rows]
    key_rows = jnp.concatenate([own_keys[: rows // 2], own_keys[rows // 2 :]], axis=1)
    packed = share(jnp.concatenate([panels_zh, key_rows], axis=0), "x", n_x)
    value_mine = packed[:, : n_zh * rows].reshape(width, half)
    key_got = packed[:, n_zh * rows :]
    keys_x = jnp.concatenate([key_got[:, :, :head], key_got[:, :, head:]], axis=1).reshape(
        n_x * rows, head
    )
    value_own = jnp.concatenate([value_mine, other_core(value_mine)], axis=1)
    queries_all = jnp.concatenate([queries_zh, other_core(queries_zh)], axis=0)
    pos_pair = jnp.stack([pos_zh, other_core(pos_zh)]).astype(F32)
    pos_all = (pos_pair[:, :, 0] * 128.0 + pos_pair[:, :, 1]).astype(jnp.int32).reshape(-1)

    count = queries_all.shape[0]
    scale = head ** (-0.5)
    core_of = own_first(jnp.arange(2, dtype=jnp.int32))
    query_index = (
        ((ix * n_zh + jnp.arange(n_zh, dtype=jnp.int32))[None, :, None] * 2 + core_of[:, None, None])
        * rows
        + jnp.arange(rows, dtype=jnp.int32)[None, None, :]
    ).reshape(-1)
    key_index = (
        ((jnp.arange(n_x, dtype=jnp.int32) * n_zh + izh) * 2 + ic)[:, None] * rows
        + jnp.arange(rows, dtype=jnp.int32)[None, :]
    ).reshape(-1)
    visible = (key_index[:, None] <= query_index[None, :]) & (
        key_index[:, None] >= (query_index - pos_all)[None, :]
    )
    masked = jnp.where(visible, contract_last(keys_x, queries_all) * scale, -jnp.inf)
    top = jnp.maximum(jnp.max(masked, axis=0), -1e30)
    total = jnp.sum(jnp.exp(masked - top[None, :]), axis=0)
    stats = jnp.stack([top, total]).reshape(2, 2, count // 2)
    stats = jnp.where(first, stats, stats[:, ::-1])
    stats = share(stats, ("zh", "c"), n_zh * 2)
    all_top = jnp.max(stats[:, 0], axis=0)
    all_total = jnp.sum(stats[:, 1] * jnp.exp(stats[:, 0] - all_top[None]), axis=0)
    log_total = own_first(all_top + jnp.log(all_total)).reshape(-1)
    attn_prob = jnp.exp(masked - log_total[None, :])
    prob_low = attn_prob.astype(BF16)

    projection = jnp.dot(tok_block, value_own, preferred_element_type=F32)
    value_vec = jnp.sum(
        projection.reshape(rows, experts, head) * value_gate[:, :, None], axis=1
    ).astype(BF16)
    values_x = share(value_vec, "x", n_x).reshape(n_x * rows, head)

    pulled = jnp.dot(grad_rows, output_full, preferred_element_type=F32)
    dattended = jnp.sum(
        pulled.reshape(rows, experts, head) * output_gate[:, :, None], axis=1
    ).astype(BF16)
    datt_zh = share(dattended, "zh", n_zh).reshape(n_zh * rows, head)
    datt_all = jnp.concatenate([datt_zh, other_core(datt_zh)], axis=0)

    dweights = contract_last(values_x, datt_all)
    delta = jnp.sum(prob_low.astype(F32) * dweights, axis=0).reshape(2, count // 2)
    delta = share(own_first(delta), ("zh", "c"), n_zh * 2)
    row_delta = own_first(jnp.sum(delta, axis=0)).reshape(-1)
    dscores = (attn_prob * (dweights - row_delta[None, :])).astype(BF16)

    key_term = jnp.dot(dscores, queries_all, preferred_element_type=F32) * scale
    value_term = jnp.dot(prob_low, datt_all, preferred_element_type=F32)
    key_value = jnp.concatenate([key_term, value_term], axis=1).astype(BF16)
    key_value = exchange(key_value.reshape(n_x, rows, 2 * head), "x")
    key_value = jnp.sum(key_value.astype(F32), axis=0).astype(BF16)
    grad_keys = key_value[:, :head]
    dvalue = key_value[:, head:]

    attended_term = contract_first(prob_low, values_x)
    query_term = contract_first(dscores, keys_x) * scale
    both = jnp.concatenate([attended_term, query_term], axis=1)
    both = both[: count // 2] + other_core(both[count // 2 :].astype(BF16)).astype(F32)
    both = exchange(both.astype(BF16).reshape(n_zh, rows, 2 * head), "zh")
    both = jnp.sum(both.astype(F32), axis=0).astype(BF16)
    attended = both[:, :head]
    grad_queries = both[:, head:]

    def expand(gate, vec):
        spread = gate[:, :, None] * vec.astype(F32)[:, None, :]
        return spread.reshape(rows, panel_width).astype(BF16)

    layer_output = contract_last(expand(output_gate, attended), output_full).astype(BF16)
    value_grad = expand(value_gate, dvalue)
    grad_tokens = contract_last(value_grad, value_own).astype(BF16)

    term_value = contract_first(tok_block, value_grad)
    term_output = contract_first(grad_rows, expand(output_gate_own, attended))
    theirs = jnp.concatenate([term_value[:, half:], term_output[:, half:]], axis=1)
    mine = jnp.concatenate([term_value[:, :half], term_output[:, :half]], axis=1)
    chip = (mine + other_core(theirs.astype(BF16)).astype(F32)).astype(BF16)
    piece = panel_rows // n_y
    chip = chip.reshape(n_x, n_zh, 2, n_y, piece, panel_width).transpose(0, 3, 1, 2, 4, 5)
    chip = exchange(chip.reshape(n_x * n_y, n_zh * 2 * piece, panel_width), ("x", "y"))
    plane = jnp.sum(chip.astype(F32), axis=0).astype(BF16)
    small = piece // n_zl
    plane = plane.reshape(n_zh, 2, n_zl, small, panel_width).transpose(2, 0, 1, 3, 4)
    plane = exchange(plane.reshape(n_zl * n_zh, 2 * small, panel_width), ("zl", "zh"))
    whole = jnp.sum(plane.astype(F32), axis=0).astype(BF16).reshape(2, small, panel_width)
    keep = lax.dynamic_index_in_dim(whole, ic, 0, keepdims=False)
    give = lax.dynamic_index_in_dim(whole, 1 - ic, 0, keepdims=False)
    whole = own_first(jnp.stack([keep, other_core(give)]))
    whole = share(whole, ("zl", "y"), n_zl * n_y)
    whole = whole.reshape(n_zl, n_y, 2, small, 2, half).transpose(4, 1, 0, 3, 2, 5)
    grads = whole.reshape(2, panel_rows, panel_width).astype(F32)
    return (
        layer_output[None],
        grad_tokens[None],
        grad_queries[None],
        grad_keys[None],
        grads[0],
        grads[1],
    )


def solution(mesh):
    chips = Mesh(mesh.devices.reshape(2, 4, 4, 4, 2), ("zl", "y", "x", "zh", "c"))
    batch, place = ("zl", "y"), ("x", "zh", "c")
    wide = P(batch, place, None)
    panel = P(place, None)
    in_specs = (wide, wide, wide, P(batch, place), wide, wide, wide, wide, panel, panel, wide)
    out_specs = (wide, wide, wide, wide, panel, panel)
    return jax.shard_map(
        body, mesh=chips, in_specs=in_specs, out_specs=out_specs, check_vma=False
    )
```

```python
import jax
import jax.numpy as jnp
from jax import lax
from jax.experimental import pallas as pl
from jax.experimental.pallas import tpu as pltpu
from jax.sharding import Mesh, PartitionSpec as P

F32 = jnp.float32
BF16 = jnp.bfloat16


def expert_gates(scores, chosen, experts):
    chosen_hit = chosen[:, :, None] == lax.iota(jnp.int32, experts)[None, None, :]
    return jnp.where(jnp.any(chosen_hit, axis=1), scores, F32(0.0))


def contract_last(left, right):
    return lax.dot_general(left, right, (((1,), (1,)), ((), ())), preferred_element_type=F32)


def contract_first(left, right):
    return lax.dot_general(left, right, (((0,), (0,)), ((), ())), preferred_element_type=F32)


def exchange(blocks, axes):
    return lax.all_to_all(blocks, axes, 0, 0, tiled=True)


def share(block, axes, count):
    return exchange(jnp.broadcast_to(block[None], (count,) + block.shape), axes)


def gather_experts(gate, panels):
    head = panels.shape[1] // gate.shape[1]
    total = F32(0.0)
    for e in range(gate.shape[1]):
        total = total + panels[:, e * head : (e + 1) * head] * gate[:, e : e + 1]
    return total.astype(BF16)


def expand(gate, vec):
    vec = vec.astype(F32)
    return jnp.concatenate(
        [(gate[:, e : e + 1] * vec).astype(BF16) for e in range(gate.shape[1])], axis=1
    )


def other_core(value):
    return lax.ppermute(value, "c", [(0, 1), (1, 0)])


def shifted(count, step):
    return [(k, (k + step) % count) for k in range(count)]


def ring_share(block, axis, count, at):
    place = lax.axis_index(axis)
    shape = block.shape[:at] + (count,) + block.shape[at:]
    result = jnp.zeros(shape, block.dtype)
    for step in range(count):
        part = lax.ppermute(block, axis, shifted(count, step)) if step else block
        part = jnp.expand_dims(part, at)
        result = lax.dynamic_update_slice_in_dim(result, part, (place - step) % count, at)
    return result


def ring_parts(blocks, axis, count):
    place = lax.axis_index(axis)
    parts = []
    for step in range(count):
        part = lax.dynamic_index_in_dim(blocks, (place + step) % count, 0, keepdims=False)
        parts.append(lax.ppermute(part, axis, shifted(count, step)) if step else part)
    return parts


def sum_bf16(parts):
    return sum(part.astype(F32) for part in parts).astype(BF16)


def ring_sum(blocks, axis, count):
    return sum_bf16(ring_parts(blocks, axis, count))


def add_bf16(left, right):
    return (left.astype(F32) + right.astype(F32)).astype(BF16)


def terms_kernel(left_ref, right_ref, mine_ref, theirs_ref):
    n_y, n_z, piece, half = mine_ref.shape[1:]
    panel = n_y * piece
    for z in range(n_z):
        out = contract_first(left_ref[:, z * panel : (z + 1) * panel], right_ref[...])
        out = out.astype(BF16).reshape(n_y, piece, 2 * half)
        mine_ref[0, :, z] = out[:, :, :half]
        theirs_ref[0, :, z] = out[:, :, half:]


def panel_terms(left, right, n_x, n_y, n_z):
    rows, width = left.shape
    half = right.shape[1] // 2
    piece = width // (n_x * n_y * n_z)
    block = (1, n_y, n_z, piece, half)
    spec = pl.BlockSpec(block, lambda x: (x, 0, 0, 0, 0))
    shape = jax.ShapeDtypeStruct((n_x,) + block[1:], BF16)
    return pl.pallas_call(
        terms_kernel,
        grid=(n_x,),
        in_specs=[
            pl.BlockSpec((rows, width // n_x), lambda x: (0, x)),
            pl.BlockSpec(right.shape, lambda x: (0, 0)),
        ],
        out_specs=[spec, spec],
        out_shape=[shape, shape],
        cost_estimate=pl.CostEstimate(
            flops=4 * rows * width * half,
            bytes_accessed=2 * rows * width + 4 * width * half,
            transcendentals=0,
        ),
        compiler_params=pltpu.CompilerParams(vmem_limit_bytes=32 * 1024 * 1024),
    )(left, right)


def body(
    tokens,
    queries,
    key_vectors,
    doc_position,
    value_scores,
    value_experts,
    output_scores,
    output_experts,
    value_panels,
    output_panels,
    cotangent,
):
    n_x, n_y, n_zh, n_zl = 4, 4, 4, 2
    tok_block = tokens[0]
    query_block = queries[0]
    own_keys = key_vectors[0]
    positions = doc_position[0]
    grad_rows = cotangent[0]
    rows, width = tok_block.shape
    head = query_block.shape[1]
    experts = value_scores.shape[2]
    panel_rows, panel_width = value_panels.shape
    half = panel_width // 2
    ix, iy = lax.axis_index("x"), lax.axis_index("y")
    izh, ic = lax.axis_index("zh"), lax.axis_index("c")
    first = ic == 0

    def own_first(pair):
        return jnp.where(first, pair, pair[::-1])

    def gate_own_first(gate):
        return own_first(gate.T.reshape(2, experts // 2, rows)).reshape(experts, rows).T

    value_gate = gate_own_first(expert_gates(value_scores[0], value_experts[0], experts))
    output_gate = gate_own_first(expert_gates(output_scores[0], output_experts[0], experts))

    mine = lax.dynamic_slice_in_dim(value_panels, ic * half, half, 1)
    theirs = lax.dynamic_slice_in_dim(value_panels, (1 - ic) * half, half, 1)
    mine_out = lax.dynamic_slice_in_dim(output_panels, ic * half, half, 1)
    theirs_out = lax.dynamic_slice_in_dim(output_panels, (1 - ic) * half, half, 1)
    mine = jnp.concatenate([mine, mine_out], axis=1)
    theirs = other_core(jnp.concatenate([theirs, theirs_out], axis=1))
    pair = own_first(jnp.stack([mine, theirs])).reshape(2 * panel_rows, 2 * half)
    value_rows = pair[:, :half]
    quarter = 2 * panel_rows // n_y
    output_rows = lax.dynamic_slice_in_dim(pair[:, half:], iy * quarter, quarter, 0)

    def fold(vecs):
        return jnp.concatenate([vecs[: rows // 2], vecs[rows // 2 :]], axis=1)

    def unfold(packed):
        return jnp.concatenate([packed[:, :, :head], packed[:, :, head:]], axis=1)

    pos_hi = (positions // 128).astype(BF16)
    pos_lo = (positions % 128).astype(BF16)
    pos_rows = jnp.zeros((16, half), BF16)
    pos_rows = pos_rows.at[0, :rows].set(pos_hi).at[1, :rows].set(pos_lo)
    packed = jnp.concatenate([output_rows, fold(query_block), pos_rows], axis=0)
    packed = share(packed, "zh", n_zh)
    output_zh = packed[:, :quarter].reshape(n_zh * quarter, half)
    queries_zh = unfold(packed[:, quarter : quarter + rows // 2]).reshape(n_zh * rows, head)
    pos_zh = packed[:, quarter + rows // 2 : quarter + rows // 2 + 2, :rows]
    packed = share(jnp.concatenate([output_zh, fold(own_keys)], axis=0), "x", n_x)
    output_x = packed[:, : n_zh * quarter].reshape(n_x, n_zh, quarter, half)
    keys_x = unfold(packed[:, n_zh * quarter :]).reshape(n_x * rows, head)
    value_zh = share(value_rows, "zh", n_zh).reshape(n_zh * 2 * panel_rows, half)
    value_mine = ring_share(value_zh, "x", n_x, 0).reshape(width, half)
    output_mine = ring_share(output_x, "y", n_y, 2).reshape(width, half)
    value_own = jnp.concatenate([value_mine, other_core(value_mine)], axis=1)
    output_own = jnp.concatenate([output_mine, other_core(output_mine)], axis=1)
    queries_all = jnp.concatenate([queries_zh, other_core(queries_zh)], axis=0)
    pos_pair = jnp.stack([pos_zh, other_core(pos_zh)]).astype(F32)
    pos_all = (pos_pair[:, :, 0] * 128.0 + pos_pair[:, :, 1]).astype(jnp.int32).reshape(-1)

    count = queries_all.shape[0]
    scale = head ** (-0.5)
    core_of = own_first(jnp.arange(2, dtype=jnp.int32))
    query_index = (
        ((ix * n_zh + jnp.arange(n_zh, dtype=jnp.int32))[None, :, None] * 2 + core_of[:, None, None])
        * rows
        + jnp.arange(rows, dtype=jnp.int32)[None, None, :]
    ).reshape(-1)
    key_index = (
        ((jnp.arange(n_x, dtype=jnp.int32) * n_zh + izh) * 2 + ic)[:, None] * rows
        + jnp.arange(rows, dtype=jnp.int32)[None, :]
    ).reshape(-1)
    visible = (key_index[:, None] <= query_index[None, :]) & (
        key_index[:, None] >= (query_index - pos_all)[None, :]
    )
    masked = jnp.where(visible, contract_last(keys_x, queries_all) * scale, -jnp.inf)
    top = jnp.maximum(jnp.max(masked, axis=0), -1e30)
    total = jnp.sum(jnp.exp(masked - top[None, :]), axis=0)
    stats = jnp.stack([top, total]).reshape(2, 2, count // 2)
    stats = jnp.where(first, stats, stats[:, ::-1])
    stats = share(stats, ("zh", "c"), n_zh * 2)
    all_top = jnp.max(stats[:, 0], axis=0)
    all_total = jnp.sum(stats[:, 1] * jnp.exp(stats[:, 0] - all_top[None]), axis=0)
    log_total = own_first(all_top + jnp.log(all_total)).reshape(-1)
    attn_prob = jnp.exp(masked - log_total[None, :])
    prob_low = attn_prob.astype(BF16)

    projection = jnp.dot(tok_block, value_own, preferred_element_type=F32)
    value_vec = gather_experts(value_gate, projection)
    values_x = ring_share(value_vec, "x", n_x, 0).reshape(n_x * rows, head)

    pulled = jnp.dot(grad_rows, output_own, preferred_element_type=F32)
    dattended = gather_experts(output_gate, pulled)
    datt_zh = share(dattended, "zh", n_zh).reshape(n_zh * rows, head)
    datt_all = jnp.concatenate([datt_zh, other_core(datt_zh)], axis=0)

    def sum_queries(term):
        return term[: count // 2] + other_core(term[count // 2 :].astype(BF16)).astype(F32)

    attended = sum_queries(contract_first(prob_low, values_x)).astype(BF16)
    attended, datt_all = lax.optimization_barrier((attended, datt_all))
    attended = exchange(attended.reshape(n_zh, rows, head), "zh")
    attended = jnp.sum(attended.astype(F32), axis=0).astype(BF16)

    dweights = contract_last(values_x, datt_all)
    delta = jnp.sum(prob_low.astype(F32) * dweights, axis=0).reshape(2, count // 2)
    delta, attended = lax.optimization_barrier((delta, attended))
    delta = share(own_first(delta), ("zh", "c"), n_zh * 2)
    row_delta = own_first(jnp.sum(delta, axis=0)).reshape(-1)
    dscores = (attn_prob * (dweights - row_delta[None, :])).astype(BF16)
    expanded = expand(output_gate, attended)

    mine, theirs = panel_terms(grad_rows, expanded, n_x, n_y, n_zh * 2)

    key_term = jnp.dot(dscores, queries_all, preferred_element_type=F32) * scale
    value_term = jnp.dot(prob_low, datt_all, preferred_element_type=F32)
    key_value = jnp.concatenate([key_term, value_term], axis=1).astype(BF16)
    chip_output = add_bf16(mine, other_core(theirs))
    parts = ring_parts(chip_output.transpose(1, 0, 2, 3, 4), "y", n_y)
    key_value, parts[1], parts[3] = lax.optimization_barrier((key_value, parts[1], parts[3]))
    key_value = exchange(key_value.reshape(n_x, rows, 2 * head), "x")
    key_value = jnp.sum(key_value.astype(F32), axis=0).astype(BF16)
    grad_keys = key_value[:, :head]
    dvalue = key_value[:, head:]
    dvalue, parts[2] = lax.optimization_barrier((dvalue, parts[2]))
    value_grad = expand(value_gate, dvalue)
    chip_output = sum_bf16(parts)

    mine, theirs = panel_terms(tok_block, value_grad, n_x, n_y, n_zh * 2)
    piece = panel_rows // n_y
    chip_value = add_bf16(mine, other_core(theirs))
    chip_value, chip_output, dscores, value_grad, expanded = lax.optimization_barrier(
        (chip_value, chip_output, dscores, value_grad, expanded)
    )
    plane_value = exchange(chip_value.reshape(n_x * n_y, n_zh * 2 * piece, half), ("x", "y"))

    plane_output = ring_sum(chip_output, "x", n_x)
    grad_queries = sum_queries(contract_first(dscores, keys_x) * scale).astype(BF16)
    grad_queries = ring_sum(grad_queries.reshape(n_zh, rows, head), "zh", n_zh)
    layer_output = contract_last(expanded, output_own).astype(BF16)
    grad_tokens = contract_last(value_grad, value_own).astype(BF16)
    plane_value, layer_output, grad_tokens, grad_queries = lax.optimization_barrier(
        (plane_value, layer_output, grad_tokens, grad_queries)
    )
    plane_value = jnp.sum(plane_value.astype(F32), axis=0).astype(BF16)
    plane = jnp.concatenate(
        [plane_value.reshape(n_zh * 2 * piece, half), plane_output.reshape(n_zh * 2 * piece, half)],
        axis=1,
    )
    small = piece // n_zl
    plane = plane.reshape(n_zh, 2, n_zl, small, panel_width).transpose(2, 0, 1, 3, 4)
    plane = exchange(plane.reshape(n_zl * n_zh, 2 * small, panel_width), ("zl", "zh"))
    whole = jnp.sum(plane.astype(F32), axis=0).astype(BF16).reshape(2, small, panel_width)
    keep = lax.dynamic_index_in_dim(whole, ic, 0, keepdims=False)
    give = lax.dynamic_index_in_dim(whole, 1 - ic, 0, keepdims=False)
    whole = own_first(jnp.stack([keep, other_core(give)]))
    whole = share(whole, ("zl", "y"), n_zl * n_y)
    whole = whole.reshape(n_zl, n_y, 2, small, 2, half).transpose(4, 1, 0, 3, 2, 5)
    grads = whole.reshape(2, panel_rows, panel_width).astype(F32)
    return (
        layer_output[None],
        grad_tokens[None],
        grad_queries[None],
        grad_keys[None],
        grads[0],
        grads[1],
    )


def solution(mesh):
    chips = Mesh(mesh.devices.reshape(2, 4, 4, 4, 2), ("zl", "y", "x", "zh", "c"))
    batch, place = ("zl", "y"), ("x", "zh", "c")
    wide = P(batch, place, None)
    panel = P(place, None)
    in_specs = (wide, wide, wide, P(batch, place), wide, wide, wide, wide, panel, panel, wide)
    out_specs = (wide, wide, wide, wide, panel, panel)
    return jax.shard_map(
        body, mesh=chips, in_specs=in_specs, out_specs=out_specs, check_vma=False
    )
```

```python
import jax
import jax.numpy as jnp
from jax import lax
from jax.experimental import pallas as pl
from jax.experimental.pallas import tpu as pltpu
from jax.sharding import Mesh, PartitionSpec as P

F32 = jnp.float32
BF16 = jnp.bfloat16


def expert_gates(scores, chosen, experts):
    chosen_hit = chosen[:, :, None] == lax.iota(jnp.int32, experts)[None, None, :]
    return jnp.where(jnp.any(chosen_hit, axis=1), scores, F32(0.0))


def contract_last(left, right):
    return lax.dot_general(left, right, (((1,), (1,)), ((), ())), preferred_element_type=F32)


def contract_first(left, right):
    return lax.dot_general(left, right, (((0,), (0,)), ((), ())), preferred_element_type=F32)


def exchange(blocks, axes):
    return lax.all_to_all(blocks, axes, 0, 0, tiled=True)


def share(block, axes, count):
    return exchange(jnp.broadcast_to(block[None], (count,) + block.shape), axes)


def gather_experts(gate, panels):
    head = panels.shape[1] // gate.shape[1]
    total = F32(0.0)
    for e in range(gate.shape[1]):
        total = total + panels[:, e * head : (e + 1) * head] * gate[:, e : e + 1]
    return total.astype(BF16)


def expand(gate, vec):
    vec = vec.astype(F32)
    return jnp.concatenate(
        [(gate[:, e : e + 1] * vec).astype(BF16) for e in range(gate.shape[1])], axis=1
    )


def other_core(value):
    return lax.ppermute(value, "c", [(0, 1), (1, 0)])


def shifted(count, step):
    return [(k, (k + step) % count) for k in range(count)]


def ring_share(block, axis, count, at):
    place = lax.axis_index(axis)
    return in_order(shifted_blocks(block, axis, count), axis, at)


def shifted_blocks(block, axis, count):
    return [block] + [lax.ppermute(block, axis, shifted(count, k)) for k in range(1, count)]


def in_order(parts, axis, at):
    place, count = lax.axis_index(axis), len(parts)
    ordered = [lax.select_n((place - member) % count, *parts) for member in range(count)]
    return jnp.stack(ordered, axis=at)


def ring_parts(blocks, axis, count):
    place = lax.axis_index(axis)
    parts = []
    for step in range(count):
        part = lax.dynamic_index_in_dim(blocks, (place + step) % count, 0, keepdims=False)
        parts.append(lax.ppermute(part, axis, shifted(count, step)) if step else part)
    return parts


def sum_bf16(parts):
    return sum(part.astype(F32) for part in parts).astype(BF16)


def ring_sum(blocks, axis, count):
    return sum_bf16(ring_parts(blocks, axis, count))


def add_bf16(left, right):
    return (left.astype(F32) + right.astype(F32)).astype(BF16)


def back_values_kernel(prob_ref, value_ref, datt_ref, delta_ref, term_ref):
    @pl.when(pl.program_id(0) == 0)
    def _():
        term_ref[...] = jnp.zeros_like(term_ref)

    keys = prob_ref.shape[0]
    step = keys // 4
    delta = F32(0.0)
    for k in range(0, keys, step):
        prob = prob_ref[k : k + step, :]
        dweights = contract_last(value_ref[k : k + step, :], datt_ref[...])
        delta = delta + jnp.sum(prob.astype(F32) * dweights, axis=0, keepdims=True)
        term_ref[k : k + step, :] += jnp.dot(prob, datt_ref[...], preferred_element_type=F32)
    delta_ref[...] = delta


def attend_back_values(prob, values, datt):
    keys, count = prob.shape
    head = values.shape[1]
    tile = count // 4
    return pl.pallas_call(
        back_values_kernel,
        grid=(4,),
        in_specs=[
            pl.BlockSpec((keys, tile), lambda j: (0, j)),
            pl.BlockSpec((keys, head), lambda j: (0, 0)),
            pl.BlockSpec((tile, head), lambda j: (j, 0)),
        ],
        out_specs=[
            pl.BlockSpec((1, tile), lambda j: (0, j)),
            pl.BlockSpec((keys, head), lambda j: (0, 0)),
        ],
        out_shape=[
            jax.ShapeDtypeStruct((1, count), F32),
            jax.ShapeDtypeStruct((keys, head), F32),
        ],
        cost_estimate=pl.CostEstimate(
            flops=4 * keys * count * head, bytes_accessed=2 * keys * count, transcendentals=0
        ),
        compiler_params=pltpu.CompilerParams(vmem_limit_bytes=32 * 1024 * 1024),
    )(prob, values, datt)


def back_scores_kernel(
    prob_ref, value_ref, datt_ref, delta_ref, query_ref, key_ref, key_term_ref, query_term_ref
):
    @pl.when(pl.program_id(0) == 0)
    def _():
        key_term_ref[...] = jnp.zeros_like(key_term_ref)

    keys = prob_ref.shape[0]
    step = keys // 4
    query_term = F32(0.0)
    for k in range(0, keys, step):
        dweights = contract_last(value_ref[k : k + step, :], datt_ref[...])
        prob = prob_ref[k : k + step, :].astype(F32)
        dscores = (prob * (dweights - delta_ref[...])).astype(BF16)
        key_term_ref[k : k + step, :] += jnp.dot(
            dscores, query_ref[...], preferred_element_type=F32
        )
        query_term = query_term + contract_first(dscores, key_ref[k : k + step, :])
    query_term_ref[...] = query_term


def attend_back_scores(prob, values, datt, delta, queries, keys_x):
    keys, count = prob.shape
    head = values.shape[1]
    tile = count // 4
    across = pl.BlockSpec((tile, head), lambda j: (j, 0))
    down = pl.BlockSpec((keys, head), lambda j: (0, 0))
    return pl.pallas_call(
        back_scores_kernel,
        grid=(4,),
        in_specs=[
            pl.BlockSpec((keys, tile), lambda j: (0, j)),
            down,
            across,
            pl.BlockSpec((1, tile), lambda j: (0, j)),
            across,
            down,
        ],
        out_specs=[down, across],
        out_shape=[
            jax.ShapeDtypeStruct((keys, head), F32),
            jax.ShapeDtypeStruct((count, head), F32),
        ],
        cost_estimate=pl.CostEstimate(
            flops=6 * keys * count * head, bytes_accessed=2 * keys * count, transcendentals=0
        ),
        compiler_params=pltpu.CompilerParams(vmem_limit_bytes=32 * 1024 * 1024),
    )(prob, values, datt, delta, queries, keys_x)


def terms_kernel(left_ref, right_ref, mine_ref, theirs_ref):
    n_y, n_z, piece, half = mine_ref.shape[1:]
    panel = n_y * piece
    for z in range(n_z):
        out = contract_first(left_ref[:, z * panel : (z + 1) * panel], right_ref[...])
        out = out.astype(BF16).reshape(n_y, piece, 2 * half)
        mine_ref[0, :, z] = out[:, :, :half]
        theirs_ref[0, :, z] = out[:, :, half:]


def panel_terms(left, right, n_x, n_y, n_z):
    rows, width = left.shape
    half = right.shape[1] // 2
    piece = width // (n_x * n_y * n_z)
    block = (1, n_y, n_z, piece, half)
    spec = pl.BlockSpec(block, lambda x: (x, 0, 0, 0, 0))
    shape = jax.ShapeDtypeStruct((n_x,) + block[1:], BF16)
    return pl.pallas_call(
        terms_kernel,
        grid=(n_x,),
        in_specs=[
            pl.BlockSpec((rows, width // n_x), lambda x: (0, x)),
            pl.BlockSpec(right.shape, lambda x: (0, 0)),
        ],
        out_specs=[spec, spec],
        out_shape=[shape, shape],
        cost_estimate=pl.CostEstimate(
            flops=4 * rows * width * half,
            bytes_accessed=2 * rows * width + 4 * width * half,
            transcendentals=0,
        ),
        compiler_params=pltpu.CompilerParams(vmem_limit_bytes=32 * 1024 * 1024),
    )(left, right)


def body(
    tokens,
    queries,
    key_vectors,
    doc_position,
    value_scores,
    value_experts,
    output_scores,
    output_experts,
    value_panels,
    output_panels,
    cotangent,
):
    n_x, n_y, n_zh, n_zl = 4, 4, 4, 2
    tok_block = tokens[0]
    query_block = queries[0]
    own_keys = key_vectors[0]
    positions = doc_position[0]
    grad_rows = cotangent[0]
    rows, width = tok_block.shape
    head = query_block.shape[1]
    experts = value_scores.shape[2]
    panel_rows, panel_width = value_panels.shape
    half = panel_width // 2
    ix, iy = lax.axis_index("x"), lax.axis_index("y")
    izh, ic = lax.axis_index("zh"), lax.axis_index("c")
    first = ic == 0

    def own_first(pair):
        return jnp.where(first, pair, pair[::-1])

    def gate_own_first(gate):
        return own_first(gate.T.reshape(2, experts // 2, rows)).reshape(experts, rows).T

    value_full = lax.all_gather(value_panels, ("x", "zh", "c"), axis=0, tiled=True)
    mine = lax.dynamic_slice_in_dim(output_panels, ic * half, half, 1)
    theirs = lax.dynamic_slice_in_dim(output_panels, (1 - ic) * half, half, 1)
    pair = own_first(jnp.stack([mine, other_core(theirs)])).reshape(2 * panel_rows, half)
    quarter = 2 * panel_rows // n_y
    output_rows = lax.dynamic_slice_in_dim(pair, iy * quarter, quarter, 0)

    def fold(vecs):
        return jnp.concatenate([vecs[: rows // 2], vecs[rows // 2 :]], axis=1)

    def unfold(packed):
        return jnp.concatenate([packed[:, :, :head], packed[:, :, head:]], axis=1)

    pos_hi = (positions // 128).astype(BF16)
    pos_lo = (positions % 128).astype(BF16)
    pos_rows = jnp.zeros((16, half), BF16)
    pos_rows = pos_rows.at[0, :rows].set(pos_hi).at[1, :rows].set(pos_lo)
    packed = jnp.concatenate([output_rows, fold(query_block), pos_rows], axis=0)
    packed = share(packed, "zh", n_zh)
    packed, vs, ve, os, oe = lax.optimization_barrier(
        (packed, value_scores[0], value_experts[0], output_scores[0], output_experts[0])
    )
    value_gate = expert_gates(vs, ve, experts)
    value_gate_own = gate_own_first(value_gate)
    output_gate = gate_own_first(expert_gates(os, oe, experts))
    output_zh = packed[:, :quarter].reshape(n_zh * quarter, half)
    queries_zh = unfold(packed[:, quarter : quarter + rows // 2]).reshape(n_zh * rows, head)
    pos_zh = packed[:, quarter + rows // 2 : quarter + rows // 2 + 2, :rows]
    packed = share(jnp.concatenate([output_zh, fold(own_keys)], axis=0), "x", n_x)
    output_x = packed[:, : n_zh * quarter].reshape(n_x, n_zh, quarter, half)
    keys_x = unfold(packed[:, n_zh * quarter :]).reshape(n_x * rows, head)
    output_parts = shifted_blocks(output_x, "y", n_y)
    queries_all = jnp.concatenate([queries_zh, other_core(queries_zh)], axis=0)
    pos_pair = jnp.stack([pos_zh, other_core(pos_zh)]).astype(F32)
    pos_all = (pos_pair[:, :, 0] * 128.0 + pos_pair[:, :, 1]).astype(jnp.int32).reshape(-1)

    count = queries_all.shape[0]
    scale = head ** (-0.5)
    core_of = own_first(jnp.arange(2, dtype=jnp.int32))
    query_index = (
        ((ix * n_zh + jnp.arange(n_zh, dtype=jnp.int32))[None, :, None] * 2 + core_of[:, None, None])
        * rows
        + jnp.arange(rows, dtype=jnp.int32)[None, None, :]
    ).reshape(-1)
    key_index = (
        ((jnp.arange(n_x, dtype=jnp.int32) * n_zh + izh) * 2 + ic)[:, None] * rows
        + jnp.arange(rows, dtype=jnp.int32)[None, :]
    ).reshape(-1)
    visible = (key_index[:, None] <= query_index[None, :]) & (
        key_index[:, None] >= (query_index - pos_all)[None, :]
    )
    masked = jnp.where(visible, contract_last(keys_x, queries_all) * scale, -jnp.inf)
    top = jnp.maximum(jnp.max(masked, axis=0), -1e30)
    total = jnp.sum(jnp.exp(masked - top[None, :]), axis=0)
    stats = jnp.stack([top, total]).reshape(2, 2, count // 2)
    stats = jnp.where(first, stats, stats[:, ::-1])
    stats, output_parts[1], output_parts[3] = lax.optimization_barrier(
        (stats, output_parts[1], output_parts[3])
    )
    stats = share(stats, ("zh", "c"), n_zh * 2)
    all_top = jnp.max(stats[:, 0], axis=0)
    all_total = jnp.sum(stats[:, 1] * jnp.exp(stats[:, 0] - all_top[None]), axis=0)
    log_total = own_first(all_top + jnp.log(all_total)).reshape(-1)
    log_total, output_parts[2] = lax.optimization_barrier((log_total, output_parts[2]))
    output_mine = in_order(output_parts, "y", 2).reshape(width, half)
    output_own = jnp.concatenate([output_mine, other_core(output_mine)], axis=1)
    prob_low = jnp.exp(masked - log_total[None, :]).astype(BF16)

    projection = jnp.dot(tok_block, value_full, preferred_element_type=F32)
    value_vec = gather_experts(value_gate, projection)
    values_x = ring_share(value_vec, "x", n_x, 0).reshape(n_x * rows, head)

    pulled = jnp.dot(grad_rows, output_own, preferred_element_type=F32)
    dattended = gather_experts(output_gate, pulled)
    datt_zh = share(dattended, "zh", n_zh).reshape(n_zh * rows, head)
    datt_all = jnp.concatenate([datt_zh, other_core(datt_zh)], axis=0)

    def sum_queries(term):
        return term[: count // 2] + other_core(term[count // 2 :].astype(BF16)).astype(F32)

    attended = sum_queries(contract_first(prob_low, values_x)).astype(BF16)
    attended, datt_all = lax.optimization_barrier((attended, datt_all))
    attended = exchange(attended.reshape(n_zh, rows, head), "zh")
    attended = jnp.sum(attended.astype(F32), axis=0).astype(BF16)

    delta, value_term = attend_back_values(prob_low, values_x, datt_all)
    delta, attended = lax.optimization_barrier((delta.reshape(2, count // 2), attended))
    delta = share(own_first(delta), ("zh", "c"), n_zh * 2)
    row_delta = own_first(jnp.sum(delta, axis=0)).reshape(1, count)
    key_term, query_term = attend_back_scores(
        prob_low, values_x, datt_all, row_delta, queries_all, keys_x
    )
    expanded = expand(output_gate, attended)

    mine, theirs = panel_terms(grad_rows, expanded, n_x, n_y, n_zh * 2)

    key_value = jnp.concatenate([(key_term * scale).astype(BF16), value_term.astype(BF16)], axis=1)
    chip_output = add_bf16(mine, other_core(theirs))
    parts = ring_parts(chip_output.transpose(1, 0, 2, 3, 4), "y", n_y)
    key_value, parts[1], parts[3] = lax.optimization_barrier((key_value, parts[1], parts[3]))
    key_value = exchange(key_value.reshape(n_x, rows, 2 * head), "x")
    key_value = jnp.sum(key_value.astype(F32), axis=0).astype(BF16)
    grad_keys = key_value[:, :head]
    dvalue = key_value[:, head:]
    dvalue, parts[2] = lax.optimization_barrier((dvalue, parts[2]))
    value_grad = expand(value_gate_own, dvalue)
    chip_output = sum_bf16(parts)

    mine, theirs = panel_terms(tok_block, value_grad, n_x, n_y, n_zh * 2)
    piece = panel_rows // n_y
    chip_value = add_bf16(mine, other_core(theirs))
    chip_value, chip_output, query_term, dvalue, expanded = lax.optimization_barrier(
        (chip_value, chip_output, query_term, dvalue, expanded)
    )
    plane_value = exchange(chip_value.reshape(n_x * n_y, n_zh * 2 * piece, half), ("x", "y"))

    plane_output = ring_sum(chip_output, "x", n_x)
    grad_queries = sum_queries(query_term * scale).astype(BF16)
    grad_queries = ring_sum(grad_queries.reshape(n_zh, rows, head), "zh", n_zh)
    layer_output = contract_last(expanded, output_own).astype(BF16)
    grad_tokens = contract_last(expand(value_gate, dvalue), value_full).astype(BF16)
    plane_value, layer_output, grad_tokens, grad_queries = lax.optimization_barrier(
        (plane_value, layer_output, grad_tokens, grad_queries)
    )
    plane_value = jnp.sum(plane_value.astype(F32), axis=0).astype(BF16)
    plane = jnp.concatenate(
        [plane_value.reshape(n_zh * 2 * piece, half), plane_output.reshape(n_zh * 2 * piece, half)],
        axis=1,
    )
    small = piece // n_zl
    plane = plane.reshape(n_zh, 2, n_zl, small, panel_width).transpose(2, 0, 1, 3, 4)
    plane = exchange(plane.reshape(n_zl * n_zh, 2 * small, panel_width), ("zl", "zh"))
    whole = jnp.sum(plane.astype(F32), axis=0).astype(BF16).reshape(2, small, panel_width)
    whole = jnp.broadcast_to(whole[None], (n_zl * n_y,) + whole.shape)
    whole = exchange(whole.reshape(n_zl * n_y * 2, small, panel_width), ("zl", "y", "c"))
    whole = whole.reshape(n_zl, n_y, 2, small, 2, half).transpose(4, 1, 0, 3, 2, 5)
    grads = whole.reshape(2, panel_rows, panel_width).astype(F32)
    return (
        layer_output[None],
        grad_tokens[None],
        grad_queries[None],
        grad_keys[None],
        grads[0],
        grads[1],
    )


def solution(mesh):
    chips = Mesh(mesh.devices.reshape(2, 4, 4, 4, 2), ("zl", "y", "x", "zh", "c"))
    batch, place = ("zl", "y"), ("x", "zh", "c")
    wide = P(batch, place, None)
    panel = P(place, None)
    in_specs = (wide, wide, wide, P(batch, place), wide, wide, wide, wide, panel, panel, wide)
    out_specs = (wide, wide, wide, wide, panel, panel)
    return jax.shard_map(
        body, mesh=chips, in_specs=in_specs, out_specs=out_specs, check_vma=False
    )
```

```python
import functools

import jax
import jax.numpy as jnp
from jax import lax
from jax.experimental import pallas as pl
from jax.experimental.pallas import tpu as pltpu
from jax.sharding import Mesh, PartitionSpec as P

F32 = jnp.float32
BF16 = jnp.bfloat16


def expert_gates(scores, chosen, experts):
    chosen_hit = chosen[:, :, None] == lax.iota(jnp.int32, experts)[None, None, :]
    return jnp.where(jnp.any(chosen_hit, axis=1), scores, F32(0.0))


def contract_last(left, right):
    return lax.dot_general(left, right, (((1,), (1,)), ((), ())), preferred_element_type=F32)


def contract_first(left, right):
    return lax.dot_general(left, right, (((0,), (0,)), ((), ())), preferred_element_type=F32)


def exchange(blocks, axes):
    return lax.all_to_all(blocks, axes, 0, 0, tiled=True)


def share(block, axes, count):
    return exchange(jnp.broadcast_to(block[None], (count,) + block.shape), axes)


def gather_experts(gate, panels):
    head = panels.shape[1] // gate.shape[1]
    total = F32(0.0)
    for e in range(gate.shape[1]):
        total = total + panels[:, e * head : (e + 1) * head] * gate[:, e : e + 1]
    return total.astype(BF16)


def expand(gate, vec):
    vec = vec.astype(F32)
    return jnp.concatenate(
        [(gate[:, e : e + 1] * vec).astype(BF16) for e in range(gate.shape[1])], axis=1
    )


def other_core(value):
    return lax.ppermute(value, "c", [(0, 1), (1, 0)])


def shifted(count, step):
    return [(k, (k + step) % count) for k in range(count)]


def ring_share(block, axis, count, at):
    place = lax.axis_index(axis)
    return in_order(shifted_blocks(block, axis, count), axis, at)


def shifted_blocks(block, axis, count):
    return [block] + [lax.ppermute(block, axis, shifted(count, k)) for k in range(1, count)]


def in_order(parts, axis, at):
    place, count = lax.axis_index(axis), len(parts)
    ordered = [lax.select_n((place - member) % count, *parts) for member in range(count)]
    return jnp.stack(ordered, axis=at)


def ring_parts(blocks, axis, count, ordered=False):
    place = lax.axis_index(axis)
    parts = [
        lax.dynamic_index_in_dim(blocks, (place + step) % count, 0, keepdims=False)
        for step in range(count)
    ]
    for step in (1, 3):
        parts[step] = lax.ppermute(parts[step], axis, shifted(count, step))
    if ordered:
        parts[1], parts[2], parts[3] = lax.optimization_barrier((parts[1], parts[2], parts[3]))
    parts[2] = lax.ppermute(parts[2], axis, shifted(count, 2))
    return parts


def sum_bf16(parts):
    return sum(part.astype(F32) for part in parts).astype(BF16)


def ring_sum(blocks, axis, count):
    return sum_bf16(ring_parts(blocks, axis, count))


def add_bf16(left, right):
    return (left.astype(F32) + right.astype(F32)).astype(BF16)


def back_values_kernel(prob_ref, weight_ref, value_ref, datt_ref, delta_ref, term_ref):
    @pl.when(pl.program_id(0) == 0)
    def _():
        term_ref[...] = jnp.zeros_like(term_ref)

    keys = prob_ref.shape[0]
    step = keys // 4
    delta = F32(0.0)
    for k in range(0, keys, step):
        prob = prob_ref[k : k + step, :].astype(F32) * weight_ref[...]
        dweights = contract_last(value_ref[k : k + step, :], datt_ref[...])
        delta = delta + jnp.sum(prob * dweights, axis=0, keepdims=True)
        term_ref[k : k + step, :] += jnp.dot(
            prob.astype(BF16), datt_ref[...], preferred_element_type=F32
        )
    delta_ref[...] = delta


def attend_back_values(prob, weight, values, datt):
    keys, count = prob.shape
    head = values.shape[1]
    tile = count // 4
    return pl.pallas_call(
        back_values_kernel,
        grid=(4,),
        in_specs=[
            pl.BlockSpec((keys, tile), lambda j: (0, j)),
            pl.BlockSpec((1, tile), lambda j: (0, j)),
            pl.BlockSpec((keys, head), lambda j: (0, 0)),
            pl.BlockSpec((tile, head), lambda j: (j, 0)),
        ],
        out_specs=[
            pl.BlockSpec((1, tile), lambda j: (0, j)),
            pl.BlockSpec((keys, head), lambda j: (0, 0)),
        ],
        out_shape=[
            jax.ShapeDtypeStruct((1, count), F32),
            jax.ShapeDtypeStruct((keys, head), F32),
        ],
        cost_estimate=pl.CostEstimate(
            flops=4 * keys * count * head, bytes_accessed=2 * keys * count, transcendentals=0
        ),
        compiler_params=pltpu.CompilerParams(vmem_limit_bytes=32 * 1024 * 1024),
    )(prob, weight, values, datt)


def back_scores_kernel(
    prob_ref,
    weight_ref,
    value_ref,
    datt_ref,
    delta_ref,
    query_ref,
    key_ref,
    key_term_ref,
    query_term_ref,
):
    @pl.when(pl.program_id(0) == 0)
    def _():
        key_term_ref[...] = jnp.zeros_like(key_term_ref)

    keys = prob_ref.shape[0]
    step = keys // 4
    query_term = F32(0.0)
    for k in range(0, keys, step):
        dweights = contract_last(value_ref[k : k + step, :], datt_ref[...])
        prob = prob_ref[k : k + step, :].astype(F32) * weight_ref[...]
        dscores = (prob * (dweights - delta_ref[...])).astype(BF16)
        key_term_ref[k : k + step, :] += jnp.dot(
            dscores, query_ref[...], preferred_element_type=F32
        )
        query_term = query_term + contract_first(dscores, key_ref[k : k + step, :])
    query_term_ref[...] = query_term


def attend_back_scores(prob, weight, values, datt, delta, queries, keys_x):
    keys, count = prob.shape
    head = values.shape[1]
    tile = count // 4
    across = pl.BlockSpec((tile, head), lambda j: (j, 0))
    down = pl.BlockSpec((keys, head), lambda j: (0, 0))
    return pl.pallas_call(
        back_scores_kernel,
        grid=(4,),
        in_specs=[
            pl.BlockSpec((keys, tile), lambda j: (0, j)),
            pl.BlockSpec((1, tile), lambda j: (0, j)),
            down,
            across,
            pl.BlockSpec((1, tile), lambda j: (0, j)),
            across,
            down,
        ],
        out_specs=[down, across],
        out_shape=[
            jax.ShapeDtypeStruct((keys, head), F32),
            jax.ShapeDtypeStruct((count, head), F32),
        ],
        cost_estimate=pl.CostEstimate(
            flops=6 * keys * count * head, bytes_accessed=2 * keys * count, transcendentals=0
        ),
        compiler_params=pltpu.CompilerParams(vmem_limit_bytes=32 * 1024 * 1024),
    )(prob, weight, values, datt, delta, queries, keys_x)


def terms_kernel(left_ref, right_ref, mine_ref, theirs_ref):
    n_y, n_z, piece, half = mine_ref.shape[1:]
    panel = n_y * piece
    for z in range(n_z):
        out = contract_first(left_ref[:, z * panel : (z + 1) * panel], right_ref[...])
        out = out.astype(BF16).reshape(n_y, piece, 2 * half)
        mine_ref[0, :, z] = out[:, :, :half]
        theirs_ref[0, :, z] = out[:, :, half:]


def panel_terms(left, right, n_x, n_y, n_z):
    rows, width = left.shape
    half = right.shape[1] // 2
    piece = width // (n_x * n_y * n_z)
    block = (1, n_y, n_z, piece, half)
    spec = pl.BlockSpec(block, lambda x: (x, 0, 0, 0, 0))
    shape = jax.ShapeDtypeStruct((n_x,) + block[1:], BF16)
    return pl.pallas_call(
        terms_kernel,
        grid=(n_x,),
        in_specs=[
            pl.BlockSpec((rows, width // n_x), lambda x: (0, x)),
            pl.BlockSpec(right.shape, lambda x: (0, 0)),
        ],
        out_specs=[spec, spec],
        out_shape=[shape, shape],
        cost_estimate=pl.CostEstimate(
            flops=4 * rows * width * half,
            bytes_accessed=2 * rows * width + 4 * width * half,
            transcendentals=0,
        ),
        compiler_params=pltpu.CompilerParams(vmem_limit_bytes=32 * 1024 * 1024),
    )(left, right)


def sum_plane_kernel(n_zl, n_zh, got_ref, out_ref):
    members, _, half = got_ref.shape
    small = out_ref.shape[1] // 2
    n_value = n_zl * n_zh * 2 * small
    n_y = 2 * n_zl
    part = small // 2
    total = F32(0.0)
    for m in range(members):
        total = total + got_ref[m, :n_value, :].astype(F32)
    total = total.astype(BF16)
    for zh in range(n_zh):
        for c in range(2):
            for zl in range(n_zl):
                row = ((zh * 2 + c) * n_zl + zl) * small
                out_ref[zl * n_zh + zh, c * small : (c + 1) * small, :half] = total[
                    row : row + small
                ]
    for zl in range(n_zl):
        sums = []
        for y in (2 * zl, 2 * zl + 1):
            total = F32(0.0)
            for x in range(members // n_y):
                total = total + got_ref[x * n_y + y, n_value:, :].astype(F32)
            sums.append(total)
        for zh in range(n_zh):
            for c in range(2):
                row = (zh * 2 + c) * part
                both = jnp.concatenate([t[row : row + part] for t in sums], axis=0)
                out_ref[zl * n_zh + zh, c * small : (c + 1) * small, half:] = both.astype(BF16)


def sum_plane(got, n_x, n_zl, n_zh):
    members, rows, half = got.shape
    small = rows * 4 // 5 // (n_zl * n_zh * 2)
    return pl.pallas_call(
        functools.partial(sum_plane_kernel, n_zl, n_zh),
        out_shape=jax.ShapeDtypeStruct((n_zl * n_zh, 2 * small, 2 * half), BF16),
        compiler_params=pltpu.CompilerParams(vmem_limit_bytes=32 * 1024 * 1024),
    )(got)


def place_rows_kernel(n_zl, n_y, got_ref, value_ref, output_ref):
    small = got_ref.shape[1]
    half = got_ref.shape[2] // 2
    part = small // 2
    for zl in range(n_zl):
        for y in range(n_y):
            for c in range(2):
                got = got_ref[(zl * n_y + y) * 2 + c].astype(F32)
                columns = slice(c * half, (c + 1) * half)
                row = (y * n_zl + zl) * small
                value_ref[row : row + small, columns] = got[:, :half]
                for k in range(2):
                    row = ((zl * 2 + k) * n_y + y) * part
                    output_ref[row : row + part, columns] = got[k * part : (k + 1) * part, half:]


def place_rows(got, n_zl, n_y):
    _, small, width = got.shape
    shape = jax.ShapeDtypeStruct((n_zl * n_y * small, width), F32)
    return pl.pallas_call(
        functools.partial(place_rows_kernel, n_zl, n_y), out_shape=[shape, shape]
    )(got)


def body(
    tokens,
    queries,
    key_vectors,
    doc_position,
    value_scores,
    value_experts,
    output_scores,
    output_experts,
    value_panels,
    output_panels,
    cotangent,
):
    n_x, n_y, n_zh, n_zl = 4, 4, 4, 2
    tok_block = tokens[0]
    query_block = queries[0]
    own_keys = key_vectors[0]
    positions = doc_position[0]
    grad_rows = cotangent[0]
    rows, width = tok_block.shape
    head = query_block.shape[1]
    experts = value_scores.shape[2]
    panel_rows, panel_width = value_panels.shape
    half = panel_width // 2
    ix, iy = lax.axis_index("x"), lax.axis_index("y")
    izh, ic = lax.axis_index("zh"), lax.axis_index("c")
    first = ic == 0

    def own_first(pair):
        return jnp.where(first, pair, pair[::-1])

    def gate_own_first(gate):
        return own_first(gate.T.reshape(2, experts // 2, rows)).reshape(experts, rows).T

    starts = (ic * half, (1 - ic) * half)
    mine, theirs = (
        jnp.concatenate(
            [lax.dynamic_slice_in_dim(p, at, half, 1) for p in (value_panels, output_panels)],
            axis=1,
        )
        for at in starts
    )
    pair = own_first(jnp.stack([mine, other_core(theirs)])).reshape(2 * panel_rows, 2 * half)
    quarter = 2 * panel_rows // n_y
    pair = lax.dynamic_slice_in_dim(pair, iy * quarter, quarter, 0)

    def fold(vecs):
        return jnp.concatenate([vecs[: rows // 2], vecs[rows // 2 :]], axis=1)

    def unfold(packed):
        return jnp.concatenate([packed[:, :, :head], packed[:, :, head:]], axis=1)

    pos_hi = (positions // 128).astype(BF16)
    pos_lo = (positions % 128).astype(BF16)
    pos_rows = jnp.zeros((16, half), BF16)
    pos_rows = pos_rows.at[0, :rows].set(pos_hi).at[1, :rows].set(pos_lo)
    packed = jnp.concatenate(
        [pair[:, :half], pair[:, half:], fold(query_block), pos_rows], axis=0
    )
    packed = share(packed, "zh", n_zh)
    packed, vs, ve, os, oe = lax.optimization_barrier(
        (packed, value_scores[0], value_experts[0], output_scores[0], output_experts[0])
    )
    value_gate = gate_own_first(expert_gates(vs, ve, experts))
    output_gate = gate_own_first(expert_gates(os, oe, experts))
    value_zh = ring_share(packed[:, :quarter], "y", n_y, 1).reshape(n_zh * n_y * quarter, half)
    packed = packed[:, quarter:]
    output_zh = packed[:, :quarter].reshape(n_zh * quarter, half)
    queries_zh = unfold(packed[:, quarter : quarter + rows // 2]).reshape(n_zh * rows, head)
    pos_zh = packed[:, quarter + rows // 2 : quarter + rows // 2 + 2, :rows]
    packed = share(jnp.concatenate([output_zh, fold(own_keys)], axis=0), "x", n_x)
    output_x = packed[:, : n_zh * quarter].reshape(n_x, n_zh, quarter, half)
    keys_x = unfold(packed[:, n_zh * quarter :]).reshape(n_x * rows, head)
    near = [
        lax.ppermute(block, axis, shifted(4, step))
        for block, axis in ((value_zh, "x"), (output_x, "y"))
        for step in (1, 3)
    ]
    queries_all = jnp.concatenate([queries_zh, other_core(queries_zh)], axis=0)
    pos_pair = jnp.stack([pos_zh, other_core(pos_zh)]).astype(F32)
    pos_all = (pos_pair[:, :, 0] * 128.0 + pos_pair[:, :, 1]).astype(jnp.int32).reshape(-1)

    count = queries_all.shape[0]
    scale = head ** (-0.5)
    core_of = own_first(jnp.arange(2, dtype=jnp.int32))
    query_index = (
        ((ix * n_zh + jnp.arange(n_zh, dtype=jnp.int32))[None, :, None] * 2 + core_of[:, None, None])
        * rows
        + jnp.arange(rows, dtype=jnp.int32)[None, None, :]
    ).reshape(-1)
    key_index = (
        ((jnp.arange(n_x, dtype=jnp.int32) * n_zh + izh) * 2 + ic)[:, None] * rows
        + jnp.arange(rows, dtype=jnp.int32)[None, :]
    ).reshape(-1)
    visible = (key_index[:, None] <= query_index[None, :]) & (
        key_index[:, None] >= (query_index - pos_all)[None, :]
    )
    masked = jnp.where(visible, contract_last(keys_x, queries_all) * scale, -jnp.inf)
    top = jnp.maximum(jnp.max(masked, axis=0), -1e30)
    total = jnp.sum(jnp.exp(masked - top[None, :]), axis=0)
    top, total, near, value_far, output_far = lax.optimization_barrier(
        (top, total, near, value_zh, output_x)
    )
    far = [
        lax.ppermute(value_far, "x", shifted(n_x, 2)),
        lax.ppermute(output_far, "y", shifted(n_y, 2)),
    ]
    prob_low = jnp.exp(masked - top[None, :]).astype(BF16)
    stats = jnp.stack([top, total]).reshape(2, 2, count // 2)
    stats = jnp.where(first, stats, stats[:, ::-1])
    stats = share(stats, ("zh", "c"), n_zh * 2)
    all_top = jnp.max(stats[:, 0], axis=0)
    all_total = jnp.sum(stats[:, 1] * jnp.exp(stats[:, 0] - all_top[None]), axis=0)
    log_total = own_first(all_top + jnp.log(all_total)).reshape(-1)
    weight = jnp.exp(top - log_total)
    weight, prob_low, far = lax.optimization_barrier((weight, prob_low, far))
    value_parts = [value_zh, near[0], far[0], near[1]]
    output_parts = [output_x, near[2], far[1], near[3]]
    value_mine = in_order(value_parts, "x", 0).reshape(width, half)
    value_own = jnp.concatenate([value_mine, other_core(value_mine)], axis=1)
    output_mine = in_order(output_parts, "y", 2).reshape(width, half)
    output_own = jnp.concatenate([output_mine, other_core(output_mine)], axis=1)

    projection = jnp.dot(tok_block, value_own, preferred_element_type=F32)
    value_vec = gather_experts(value_gate, projection)
    values_x = ring_share(value_vec, "x", n_x, 0).reshape(n_x * rows, head)

    pulled = jnp.dot(grad_rows, output_own, preferred_element_type=F32)
    dattended = gather_experts(output_gate, pulled)
    datt_zh = share(dattended, "zh", n_zh).reshape(n_zh * rows, head)
    datt_all = jnp.concatenate([datt_zh, other_core(datt_zh)], axis=0)

    def sum_queries(term):
        return term[: count // 2] + other_core(term[count // 2 :].astype(BF16)).astype(F32)

    attended = contract_first(prob_low, values_x) * weight[:, None]
    attended = sum_queries(attended).astype(BF16)
    attended, datt_all = lax.optimization_barrier((attended, datt_all))
    attended = ring_sum(attended.reshape(n_zh, rows, head), "zh", n_zh)

    weight = weight.reshape(1, count)
    delta, value_term = attend_back_values(prob_low, weight, values_x, datt_all)
    delta = delta.reshape(2, count // 2)
    delta = share(own_first(delta), ("zh", "c"), n_zh * 2)
    row_delta = own_first(jnp.sum(delta, axis=0)).reshape(1, count)
    expanded = expand(output_gate, attended)

    mine, theirs = panel_terms(grad_rows, expanded, n_x, n_y, n_zh * 2)
    row_delta, theirs = lax.optimization_barrier((row_delta, theirs))
    key_term, query_term = attend_back_scores(
        prob_low, weight, values_x, datt_all, row_delta, queries_all, keys_x
    )

    key_value = jnp.concatenate([(key_term * scale).astype(BF16), value_term.astype(BF16)], axis=1)
    chip_output = add_bf16(mine, other_core(theirs))
    parts = ring_parts(chip_output.transpose(1, 0, 2, 3, 4), "y", n_y, ordered=True)
    key_value, parts[1], parts[3] = lax.optimization_barrier((key_value, parts[1], parts[3]))
    key_value = exchange(key_value.reshape(n_x, rows, 2 * head), "x")
    key_value = jnp.sum(key_value.astype(F32), axis=0).astype(BF16)
    grad_keys = key_value[:, :head]
    dvalue = key_value[:, head:]
    dvalue, parts[2] = lax.optimization_barrier((dvalue, parts[2]))
    chip_output = sum_bf16(parts)
    value_grad = expand(value_gate, dvalue)

    mine, theirs = panel_terms(tok_block, value_grad, n_x, n_y, n_zh * 2)
    piece = panel_rows // n_y
    part = piece // n_y
    chip_value = add_bf16(mine, other_core(theirs))
    chip_value, query_term, value_grad, expanded = lax.optimization_barrier(
        (chip_value, query_term, value_grad, expanded)
    )
    chip_value = chip_value.reshape(n_x * n_y, n_zh * 2 * piece, half)
    chip_output = chip_output.reshape(n_x, n_zh * 2, n_y, part, half).transpose(0, 2, 1, 3, 4)
    chip_output = chip_output.reshape(n_x * n_y, n_zh * 2 * part, half)
    plane = exchange(jnp.concatenate([chip_value, chip_output], axis=1), ("x", "y"))

    grad_queries = sum_queries(query_term * scale).astype(BF16)
    grad_queries = ring_sum(grad_queries.reshape(n_zh, rows, head), "zh", n_zh)
    layer_output = contract_last(expanded, output_own).astype(BF16)
    grad_tokens = contract_last(value_grad, value_own).astype(BF16)
    plane, layer_output, grad_tokens, grad_queries = lax.optimization_barrier(
        (plane, layer_output, grad_tokens, grad_queries)
    )
    small = piece // n_zl
    plane = sum_plane(plane, n_x, n_zl, n_zh)
    plane = exchange(plane, ("zl", "zh"))
    whole = jnp.sum(plane.astype(F32), axis=0).astype(BF16).reshape(2, small, panel_width)
    whole = jnp.broadcast_to(whole[None], (n_zl * n_y,) + whole.shape)
    whole = exchange(whole.reshape(n_zl * n_y * 2, small, panel_width), ("zl", "y", "c"))
    grad_value, grad_output = place_rows(whole, n_zl, n_y)
    return (
        layer_output[None],
        grad_tokens[None],
        grad_queries[None],
        grad_keys[None],
        grad_value,
        grad_output,
    )


def solution(mesh):
    chips = Mesh(mesh.devices.reshape(2, 4, 4, 4, 2), ("zl", "y", "x", "zh", "c"))
    batch, place = ("zl", "y"), ("x", "zh", "c")
    wide = P(batch, place, None)
    panel = P(place, None)
    in_specs = (wide, wide, wide, P(batch, place), wide, wide, wide, wide, panel, panel, wide)
    out_specs = (wide, wide, wide, wide, panel, panel)
    return jax.shard_map(
        body, mesh=chips, in_specs=in_specs, out_specs=out_specs, check_vma=False
    )
```

```python
import functools

import jax
import jax.numpy as jnp
from jax import lax
from jax.experimental import pallas as pl
from jax.experimental.pallas import tpu as pltpu
from jax.sharding import Mesh, PartitionSpec as P

F32 = jnp.float32
BF16 = jnp.bfloat16


def expert_gates(scores, chosen, experts):
    chosen_hit = chosen[:, :, None] == lax.iota(jnp.int32, experts)[None, None, :]
    return jnp.where(jnp.any(chosen_hit, axis=1), scores, F32(0.0))


def contract_last(left, right):
    return lax.dot_general(left, right, (((1,), (1,)), ((), ())), preferred_element_type=F32)


def contract_first(left, right):
    return lax.dot_general(left, right, (((0,), (0,)), ((), ())), preferred_element_type=F32)


def exchange(blocks, axes):
    return lax.all_to_all(blocks, axes, 0, 0, tiled=True)


def share(block, axes, count):
    return exchange(jnp.broadcast_to(block[None], (count,) + block.shape), axes)


def gather_experts(gate, panels):
    head = panels.shape[1] // gate.shape[1]
    total = F32(0.0)
    for e in range(gate.shape[1]):
        total = total + panels[:, e * head : (e + 1) * head] * gate[:, e : e + 1]
    return total.astype(BF16)


def expand(gate, vec):
    vec = vec.astype(F32)
    return jnp.concatenate(
        [(gate[:, e : e + 1] * vec).astype(BF16) for e in range(gate.shape[1])], axis=1
    )


def other_core(value):
    return lax.ppermute(value, "c", [(0, 1), (1, 0)])


def shifted(count, step):
    return [(k, (k + step) % count) for k in range(count)]


def ring_share(block, axis, count, at):
    place = lax.axis_index(axis)
    return in_order(shifted_blocks(block, axis, count), axis, at)


def shifted_blocks(block, axis, count):
    return [block] + [lax.ppermute(block, axis, shifted(count, k)) for k in range(1, count)]


def in_order(parts, axis, at):
    place, count = lax.axis_index(axis), len(parts)
    ordered = [lax.select_n((place - member) % count, *parts) for member in range(count)]
    return jnp.stack(ordered, axis=at)


def ring_parts(blocks, axis, count, ordered=False):
    place = lax.axis_index(axis)
    parts = [
        lax.dynamic_index_in_dim(blocks, (place + step) % count, 0, keepdims=False)
        for step in range(count)
    ]
    for step in (1, 3):
        parts[step] = lax.ppermute(parts[step], axis, shifted(count, step))
    if ordered:
        parts[1], parts[2], parts[3] = lax.optimization_barrier((parts[1], parts[2], parts[3]))
    parts[2] = lax.ppermute(parts[2], axis, shifted(count, 2))
    return parts


def sum_bf16(parts):
    return sum(part.astype(F32) for part in parts).astype(BF16)


def ring_sum(blocks, axis, count):
    return sum_bf16(ring_parts(blocks, axis, count))


def add_bf16(left, right):
    return (left.astype(F32) + right.astype(F32)).astype(BF16)


def back_values_kernel(prob_ref, weight_ref, value_ref, datt_ref, delta_ref, term_ref):
    @pl.when(pl.program_id(0) == 0)
    def _():
        term_ref[...] = jnp.zeros_like(term_ref)

    keys = prob_ref.shape[0]
    step = keys // 4
    delta = F32(0.0)
    for k in range(0, keys, step):
        prob = prob_ref[k : k + step, :].astype(F32) * weight_ref[...]
        dweights = contract_last(value_ref[k : k + step, :], datt_ref[...])
        delta = delta + jnp.sum(prob * dweights, axis=0, keepdims=True)
        term_ref[k : k + step, :] += jnp.dot(
            prob.astype(BF16), datt_ref[...], preferred_element_type=F32
        )
    delta_ref[...] = delta


def attend_back_values(prob, weight, values, datt):
    keys, count = prob.shape
    head = values.shape[1]
    tile = count // 4
    return pl.pallas_call(
        back_values_kernel,
        grid=(4,),
        in_specs=[
            pl.BlockSpec((keys, tile), lambda j: (0, j)),
            pl.BlockSpec((1, tile), lambda j: (0, j)),
            pl.BlockSpec((keys, head), lambda j: (0, 0)),
            pl.BlockSpec((tile, head), lambda j: (j, 0)),
        ],
        out_specs=[
            pl.BlockSpec((1, tile), lambda j: (0, j)),
            pl.BlockSpec((keys, head), lambda j: (0, 0)),
        ],
        out_shape=[
            jax.ShapeDtypeStruct((1, count), F32),
            jax.ShapeDtypeStruct((keys, head), F32),
        ],
        cost_estimate=pl.CostEstimate(
            flops=4 * keys * count * head, bytes_accessed=2 * keys * count, transcendentals=0
        ),
        compiler_params=pltpu.CompilerParams(vmem_limit_bytes=32 * 1024 * 1024),
    )(prob, weight, values, datt)


def back_scores_kernel(
    prob_ref,
    weight_ref,
    value_ref,
    datt_ref,
    delta_ref,
    query_ref,
    key_ref,
    key_term_ref,
    query_term_ref,
):
    @pl.when(pl.program_id(0) == 0)
    def _():
        key_term_ref[...] = jnp.zeros_like(key_term_ref)

    keys = prob_ref.shape[0]
    step = keys // 4
    query_term = F32(0.0)
    for k in range(0, keys, step):
        dweights = contract_last(value_ref[k : k + step, :], datt_ref[...])
        prob = prob_ref[k : k + step, :].astype(F32) * weight_ref[...]
        dscores = (prob * (dweights - delta_ref[...])).astype(BF16)
        key_term_ref[k : k + step, :] += jnp.dot(
            dscores, query_ref[...], preferred_element_type=F32
        )
        query_term = query_term + contract_first(dscores, key_ref[k : k + step, :])
    query_term_ref[...] = query_term


def attend_back_scores(prob, weight, values, datt, delta, queries, keys_x):
    keys, count = prob.shape
    head = values.shape[1]
    tile = count // 4
    across = pl.BlockSpec((tile, head), lambda j: (j, 0))
    down = pl.BlockSpec((keys, head), lambda j: (0, 0))
    return pl.pallas_call(
        back_scores_kernel,
        grid=(4,),
        in_specs=[
            pl.BlockSpec((keys, tile), lambda j: (0, j)),
            pl.BlockSpec((1, tile), lambda j: (0, j)),
            down,
            across,
            pl.BlockSpec((1, tile), lambda j: (0, j)),
            across,
            down,
        ],
        out_specs=[down, across],
        out_shape=[
            jax.ShapeDtypeStruct((keys, head), F32),
            jax.ShapeDtypeStruct((count, head), F32),
        ],
        cost_estimate=pl.CostEstimate(
            flops=6 * keys * count * head, bytes_accessed=2 * keys * count, transcendentals=0
        ),
        compiler_params=pltpu.CompilerParams(vmem_limit_bytes=32 * 1024 * 1024),
    )(prob, weight, values, datt, delta, queries, keys_x)


def terms_kernel(left_ref, right_ref, mine_ref, theirs_ref):
    n_y, n_z, piece, half = mine_ref.shape[1:]
    panel = n_y * piece
    for z in range(n_z):
        out = contract_first(left_ref[:, z * panel : (z + 1) * panel], right_ref[...])
        out = out.astype(BF16).reshape(n_y, piece, 2 * half)
        mine_ref[0, :, z] = out[:, :, :half]
        theirs_ref[0, :, z] = out[:, :, half:]


def panel_terms(left, right, n_x, n_y, n_z):
    rows, width = left.shape
    half = right.shape[1] // 2
    piece = width // (n_x * n_y * n_z)
    block = (1, n_y, n_z, piece, half)
    spec = pl.BlockSpec(block, lambda x: (x, 0, 0, 0, 0))
    shape = jax.ShapeDtypeStruct((n_x,) + block[1:], BF16)
    return pl.pallas_call(
        terms_kernel,
        grid=(n_x,),
        in_specs=[
            pl.BlockSpec((rows, width // n_x), lambda x: (0, x)),
            pl.BlockSpec(right.shape, lambda x: (0, 0)),
        ],
        out_specs=[spec, spec],
        out_shape=[shape, shape],
        cost_estimate=pl.CostEstimate(
            flops=4 * rows * width * half,
            bytes_accessed=2 * rows * width + 4 * width * half,
            transcendentals=0,
        ),
        compiler_params=pltpu.CompilerParams(vmem_limit_bytes=32 * 1024 * 1024),
    )(left, right)


def sum_plane_kernel(n_zl, n_zh, got_ref, out_ref):
    members, _, half = got_ref.shape
    small = out_ref.shape[1] // 2
    n_value = n_zl * n_zh * 2 * small
    n_y = 2 * n_zl
    part = small // 2
    total = F32(0.0)
    for m in range(members):
        total = total + got_ref[m, :n_value, :].astype(F32)
    total = total.astype(BF16)
    for zh in range(n_zh):
        for c in range(2):
            for zl in range(n_zl):
                row = ((zh * 2 + c) * n_zl + zl) * small
                out_ref[zl * n_zh + zh, c * small : (c + 1) * small, :half] = total[
                    row : row + small
                ]
    for zl in range(n_zl):
        sums = []
        for y in (2 * zl, 2 * zl + 1):
            total = F32(0.0)
            for x in range(members // n_y):
                total = total + got_ref[x * n_y + y, n_value:, :].astype(F32)
            sums.append(total)
        for zh in range(n_zh):
            for c in range(2):
                row = (zh * 2 + c) * part
                both = jnp.concatenate([t[row : row + part] for t in sums], axis=0)
                out_ref[zl * n_zh + zh, c * small : (c + 1) * small, half:] = both.astype(BF16)


def sum_plane(got, n_x, n_zl, n_zh):
    members, rows, half = got.shape
    small = rows * 4 // 5 // (n_zl * n_zh * 2)
    return pl.pallas_call(
        functools.partial(sum_plane_kernel, n_zl, n_zh),
        out_shape=jax.ShapeDtypeStruct((n_zl * n_zh, 2 * small, 2 * half), BF16),
        compiler_params=pltpu.CompilerParams(vmem_limit_bytes=32 * 1024 * 1024),
    )(got)


def place_rows_kernel(n_zl, n_y, got_ref, value_ref, output_ref):
    small = got_ref.shape[1]
    half = got_ref.shape[2] // 2
    part = small // 2
    for zl in range(n_zl):
        for y in range(n_y):
            for c in range(2):
                got = got_ref[(zl * n_y + y) * 2 + c].astype(F32)
                columns = slice(c * half, (c + 1) * half)
                row = (y * n_zl + zl) * small
                value_ref[row : row + small, columns] = got[:, :half]
                for k in range(2):
                    row = ((zl * 2 + k) * n_y + y) * part
                    output_ref[row : row + part, columns] = got[k * part : (k + 1) * part, half:]


def place_rows(got, n_zl, n_y):
    _, small, width = got.shape
    shape = jax.ShapeDtypeStruct((n_zl * n_y * small, width), F32)
    return pl.pallas_call(
        functools.partial(place_rows_kernel, n_zl, n_y), out_shape=[shape, shape]
    )(got)


def body(
    tokens,
    queries,
    key_vectors,
    doc_position,
    value_scores,
    value_experts,
    output_scores,
    output_experts,
    value_panels,
    output_panels,
    cotangent,
):
    n_x, n_y, n_zh, n_zl = 4, 4, 4, 2
    tok_block = tokens[0]
    query_block = queries[0]
    own_keys = key_vectors[0]
    positions = doc_position[0]
    grad_rows = cotangent[0]
    rows, width = tok_block.shape
    head = query_block.shape[1]
    experts = value_scores.shape[2]
    panel_rows, panel_width = value_panels.shape
    half = panel_width // 2
    ix, iy = lax.axis_index("x"), lax.axis_index("y")
    izh, ic = lax.axis_index("zh"), lax.axis_index("c")
    first = ic == 0

    def own_first(pair):
        return jnp.where(first, pair, pair[::-1])

    def gate_own_first(gate):
        return own_first(gate.T.reshape(2, experts // 2, rows)).reshape(experts, rows).T

    starts = (ic * half, (1 - ic) * half)
    mine, theirs = (
        jnp.concatenate(
            [lax.dynamic_slice_in_dim(p, at, half, 1) for p in (value_panels, output_panels)],
            axis=1,
        )
        for at in starts
    )
    pair = own_first(jnp.stack([mine, other_core(theirs)])).reshape(2 * panel_rows, 2 * half)
    quarter = 2 * panel_rows // n_y
    pair = lax.dynamic_slice_in_dim(pair, iy * quarter, quarter, 0)

    def fold(vecs):
        return jnp.concatenate([vecs[: rows // 2], vecs[rows // 2 :]], axis=1)

    def unfold(packed):
        return jnp.concatenate([packed[:, :, :head], packed[:, :, head:]], axis=1)

    pos_hi = (positions // 128).astype(BF16)
    pos_lo = (positions % 128).astype(BF16)
    pos_rows = jnp.zeros((16, half), BF16)
    pos_rows = pos_rows.at[0, :rows].set(pos_hi).at[1, :rows].set(pos_lo)
    packed = jnp.concatenate(
        [pair[:, :half], pair[:, half:], fold(query_block), pos_rows], axis=0
    )
    packed = share(packed, "zh", n_zh)
    packed, vs, ve, os, oe = lax.optimization_barrier(
        (packed, value_scores[0], value_experts[0], output_scores[0], output_experts[0])
    )
    value_gate = gate_own_first(expert_gates(vs, ve, experts))
    output_gate = gate_own_first(expert_gates(os, oe, experts))
    value_zh = ring_share(packed[:, :quarter], "y", n_y, 1).reshape(n_zh * n_y * quarter, half)
    packed = packed[:, quarter:]
    output_zh = packed[:, :quarter].reshape(n_zh * quarter, half)
    queries_zh = unfold(packed[:, quarter : quarter + rows // 2]).reshape(n_zh * rows, head)
    pos_zh = packed[:, quarter + rows // 2 : quarter + rows // 2 + 2, :rows]
    packed = share(jnp.concatenate([output_zh, fold(own_keys)], axis=0), "x", n_x)
    output_x = packed[:, : n_zh * quarter].reshape(n_x, n_zh, quarter, half)
    keys_x = unfold(packed[:, n_zh * quarter :]).reshape(n_x * rows, head)
    value_parts = [value_zh] * n_x
    for step in (1, 3):
        value_parts[step] = lax.ppermute(value_zh, "x", shifted(n_x, step))
    value_parts[1:] = lax.optimization_barrier(value_parts[1:])
    value_parts[2] = lax.ppermute(value_parts[2], "x", shifted(n_x, 2))
    output_parts = shifted_blocks(output_x, "y", n_y)
    queries_all = jnp.concatenate([queries_zh, other_core(queries_zh)], axis=0)
    pos_pair = jnp.stack([pos_zh, other_core(pos_zh)]).astype(F32)
    pos_all = (pos_pair[:, :, 0] * 128.0 + pos_pair[:, :, 1]).astype(jnp.int32).reshape(-1)

    count = queries_all.shape[0]
    scale = head ** (-0.5)
    core_of = own_first(jnp.arange(2, dtype=jnp.int32))
    query_index = (
        ((ix * n_zh + jnp.arange(n_zh, dtype=jnp.int32))[None, :, None] * 2 + core_of[:, None, None])
        * rows
        + jnp.arange(rows, dtype=jnp.int32)[None, None, :]
    ).reshape(-1)
    key_index = (
        ((jnp.arange(n_x, dtype=jnp.int32) * n_zh + izh) * 2 + ic)[:, None] * rows
        + jnp.arange(rows, dtype=jnp.int32)[None, :]
    ).reshape(-1)
    visible = (key_index[:, None] <= query_index[None, :]) & (
        key_index[:, None] >= (query_index - pos_all)[None, :]
    )
    masked = jnp.where(visible, contract_last(keys_x, queries_all) * scale, -jnp.inf)
    top = jnp.maximum(jnp.max(masked, axis=0), -1e30)
    total = jnp.sum(jnp.exp(masked - top[None, :]), axis=0)
    prob_low = jnp.exp(masked - top[None, :]).astype(BF16)
    top, total, prob_low, value_parts, output_parts = lax.optimization_barrier(
        (top, total, prob_low, value_parts, output_parts)
    )
    stats = jnp.stack([top, total]).reshape(2, 2, count // 2)
    stats = jnp.where(first, stats, stats[:, ::-1])
    stats = share(stats, ("zh", "c"), n_zh * 2)
    all_top = jnp.max(stats[:, 0], axis=0)
    all_total = jnp.sum(stats[:, 1] * jnp.exp(stats[:, 0] - all_top[None]), axis=0)
    log_total = own_first(all_top + jnp.log(all_total)).reshape(-1)
    weight = jnp.exp(top - log_total)
    value_mine = in_order(value_parts, "x", 0).reshape(width, half)
    value_own = jnp.concatenate([value_mine, other_core(value_mine)], axis=1)
    output_mine = in_order(output_parts, "y", 2).reshape(width, half)
    output_own = jnp.concatenate([output_mine, other_core(output_mine)], axis=1)

    projection = jnp.dot(tok_block, value_own, preferred_element_type=F32)
    value_vec = gather_experts(value_gate, projection)
    values_x = ring_share(value_vec, "x", n_x, 0).reshape(n_x * rows, head)

    pulled = jnp.dot(grad_rows, output_own, preferred_element_type=F32)
    dattended = gather_experts(output_gate, pulled)
    datt_zh = ring_share(dattended, "zh", n_zh, 0).reshape(n_zh * rows, head)
    datt_all = jnp.concatenate([datt_zh, other_core(datt_zh)], axis=0)

    def sum_queries(term):
        return term[: count // 2] + other_core(term[count // 2 :].astype(BF16)).astype(F32)

    attended = contract_first(prob_low, values_x) * weight[:, None]
    attended = sum_queries(attended).astype(BF16)
    attended, datt_all = lax.optimization_barrier((attended, datt_all))
    attended = sum_bf16(list(exchange(attended.reshape(n_zh, rows, head), "zh")))

    weight = weight.reshape(1, count)
    delta, value_term = attend_back_values(prob_low, weight, values_x, datt_all)
    delta, attended = lax.optimization_barrier((delta.reshape(2, count // 2), attended))
    delta = share(own_first(delta), ("zh", "c"), n_zh * 2)
    row_delta = own_first(jnp.sum(delta, axis=0)).reshape(1, count)
    expanded = expand(output_gate, attended)

    mine, theirs = panel_terms(grad_rows, expanded, n_x, n_y, n_zh * 2)
    chip_output = add_bf16(mine, other_core(theirs))
    row_delta, chip_output = lax.optimization_barrier((row_delta, chip_output))
    key_term, query_term = attend_back_scores(
        prob_low, weight, values_x, datt_all, row_delta, queries_all, keys_x
    )

    key_value = jnp.concatenate([(key_term * scale).astype(BF16), value_term.astype(BF16)], axis=1)
    parts = ring_parts(chip_output.transpose(1, 0, 2, 3, 4), "y", n_y, ordered=True)
    key_value, parts[1], parts[3] = lax.optimization_barrier((key_value, parts[1], parts[3]))
    key_value = exchange(key_value.reshape(n_x, rows, 2 * head), "x")
    key_value = jnp.sum(key_value.astype(F32), axis=0).astype(BF16)
    grad_keys = key_value[:, :head]
    dvalue = key_value[:, head:]
    dvalue, parts[2] = lax.optimization_barrier((dvalue, parts[2]))
    chip_output = sum_bf16(parts)
    value_grad = expand(value_gate, dvalue)

    mine, theirs = panel_terms(tok_block, value_grad, n_x, n_y, n_zh * 2)
    piece = panel_rows // n_y
    part = piece // n_y
    chip_value = add_bf16(mine, other_core(theirs))
    chip_value, query_term, value_grad, expanded = lax.optimization_barrier(
        (chip_value, query_term, value_grad, expanded)
    )
    chip_value = chip_value.reshape(n_x * n_y, n_zh * 2 * piece, half)
    chip_output = chip_output.reshape(n_x, n_zh * 2, n_y, part, half).transpose(0, 2, 1, 3, 4)
    chip_output = chip_output.reshape(n_x * n_y, n_zh * 2 * part, half)
    plane = exchange(jnp.concatenate([chip_value, chip_output], axis=1), ("x", "y"))

    grad_queries = sum_queries(query_term * scale).astype(BF16)
    grad_queries = ring_sum(grad_queries.reshape(n_zh, rows, head), "zh", n_zh)
    layer_output = contract_last(expanded, output_own).astype(BF16)
    grad_tokens = contract_last(value_grad, value_own).astype(BF16)
    plane, layer_output, grad_tokens, grad_queries = lax.optimization_barrier(
        (plane, layer_output, grad_tokens, grad_queries)
    )
    small = piece // n_zl
    plane = sum_plane(plane, n_x, n_zl, n_zh)
    plane = exchange(plane, ("zl", "zh"))
    whole = jnp.sum(plane.astype(F32), axis=0).astype(BF16).reshape(2, small, panel_width)
    whole = jnp.broadcast_to(whole[None], (n_zl * n_y,) + whole.shape)
    whole = exchange(whole.reshape(n_zl * n_y * 2, small, panel_width), ("zl", "y", "c"))
    grad_value, grad_output = place_rows(whole, n_zl, n_y)
    return (
        layer_output[None],
        grad_tokens[None],
        grad_queries[None],
        grad_keys[None],
        grad_value,
        grad_output,
    )


def solution(mesh):
    chips = Mesh(mesh.devices.reshape(2, 4, 4, 4, 2), ("zl", "y", "x", "zh", "c"))
    batch, place = ("zl", "y"), ("x", "zh", "c")
    wide = P(batch, place, None)
    panel = P(place, None)
    in_specs = (wide, wide, wide, P(batch, place), wide, wide, wide, wide, panel, panel, wide)
    out_specs = (wide, wide, wide, wide, panel, panel)
    return jax.shard_map(
        body, mesh=chips, in_specs=in_specs, out_specs=out_specs, check_vma=False
    )
```

```python
import functools

import jax
import jax.numpy as jnp
from jax import lax
from jax.experimental import pallas as pl
from jax.experimental.pallas import tpu as pltpu
from jax.sharding import Mesh, PartitionSpec as P

F32 = jnp.float32
BF16 = jnp.bfloat16


def expert_gates(scores, chosen, experts):
    chosen_hit = chosen[:, :, None] == lax.iota(jnp.int32, experts)[None, None, :]
    return jnp.where(jnp.any(chosen_hit, axis=1), scores, F32(0.0))


def contract_last(left, right):
    return lax.dot_general(left, right, (((1,), (1,)), ((), ())), preferred_element_type=F32)


def contract_first(left, right):
    return lax.dot_general(left, right, (((0,), (0,)), ((), ())), preferred_element_type=F32)


def exchange(blocks, axes):
    return lax.all_to_all(blocks, axes, 0, 0, tiled=True)


def share(block, axes, count):
    return exchange(jnp.broadcast_to(block[None], (count,) + block.shape), axes)


def gather_experts(gate, panels):
    head = panels.shape[1] // gate.shape[1]
    total = F32(0.0)
    for e in range(gate.shape[1]):
        total = total + panels[:, e * head : (e + 1) * head] * gate[:, e : e + 1]
    return total.astype(BF16)


def expand(gate, vec):
    vec = vec.astype(F32)
    return jnp.concatenate(
        [(gate[:, e : e + 1] * vec).astype(BF16) for e in range(gate.shape[1])], axis=1
    )


def other_core(value):
    return lax.ppermute(value, "c", [(0, 1), (1, 0)])


def shifted(count, step):
    return [(k, (k + step) % count) for k in range(count)]


def ring_share(block, axis, count, at):
    place = lax.axis_index(axis)
    return in_order(shifted_blocks(block, axis, count), axis, at)


def shifted_blocks(block, axis, count):
    return [block] + [lax.ppermute(block, axis, shifted(count, k)) for k in range(1, count)]


def in_order(parts, axis, at):
    place, count = lax.axis_index(axis), len(parts)
    ordered = [lax.select_n((place - member) % count, *parts) for member in range(count)]
    return jnp.stack(ordered, axis=at)


def ring_parts(blocks, axis, count, ordered=False):
    place = lax.axis_index(axis)
    parts = [
        lax.dynamic_index_in_dim(blocks, (place + step) % count, 0, keepdims=False)
        for step in range(count)
    ]
    for step in (1, 3):
        parts[step] = lax.ppermute(parts[step], axis, shifted(count, step))
    if ordered:
        parts[1], parts[2], parts[3] = lax.optimization_barrier((parts[1], parts[2], parts[3]))
    parts[2] = lax.ppermute(parts[2], axis, shifted(count, 2))
    return parts


def sum_bf16(parts):
    return sum(part.astype(F32) for part in parts).astype(BF16)


def ring_sum(blocks, axis, count):
    return sum_bf16(ring_parts(blocks, axis, count))


def add_bf16(left, right):
    return (left.astype(F32) + right.astype(F32)).astype(BF16)


def back_values_kernel(prob_ref, weight_ref, value_ref, datt_ref, delta_ref, term_ref):
    @pl.when(pl.program_id(0) == 0)
    def _():
        term_ref[...] = jnp.zeros_like(term_ref)

    keys = prob_ref.shape[0]
    step = keys // 4
    delta = F32(0.0)
    for k in range(0, keys, step):
        prob = prob_ref[k : k + step, :].astype(F32) * weight_ref[...]
        dweights = contract_last(value_ref[k : k + step, :], datt_ref[...])
        delta = delta + jnp.sum(prob * dweights, axis=0, keepdims=True)
        term_ref[k : k + step, :] += jnp.dot(
            prob.astype(BF16), datt_ref[...], preferred_element_type=F32
        )
    delta_ref[...] = delta


def attend_back_values(prob, weight, values, datt):
    keys, count = prob.shape
    head = values.shape[1]
    tile = count // 4
    return pl.pallas_call(
        back_values_kernel,
        grid=(4,),
        in_specs=[
            pl.BlockSpec((keys, tile), lambda j: (0, j)),
            pl.BlockSpec((1, tile), lambda j: (0, j)),
            pl.BlockSpec((keys, head), lambda j: (0, 0)),
            pl.BlockSpec((tile, head), lambda j: (j, 0)),
        ],
        out_specs=[
            pl.BlockSpec((1, tile), lambda j: (0, j)),
            pl.BlockSpec((keys, head), lambda j: (0, 0)),
        ],
        out_shape=[
            jax.ShapeDtypeStruct((1, count), F32),
            jax.ShapeDtypeStruct((keys, head), F32),
        ],
        cost_estimate=pl.CostEstimate(
            flops=4 * keys * count * head, bytes_accessed=2 * keys * count, transcendentals=0
        ),
        compiler_params=pltpu.CompilerParams(vmem_limit_bytes=32 * 1024 * 1024),
    )(prob, weight, values, datt)


def back_scores_kernel(
    prob_ref,
    weight_ref,
    value_ref,
    datt_ref,
    delta_ref,
    query_ref,
    key_ref,
    key_term_ref,
    query_term_ref,
):
    @pl.when(pl.program_id(0) == 0)
    def _():
        key_term_ref[...] = jnp.zeros_like(key_term_ref)

    keys = prob_ref.shape[0]
    step = keys // 4
    query_term = F32(0.0)
    for k in range(0, keys, step):
        dweights = contract_last(value_ref[k : k + step, :], datt_ref[...])
        prob = prob_ref[k : k + step, :].astype(F32) * weight_ref[...]
        dscores = (prob * (dweights - delta_ref[...])).astype(BF16)
        key_term_ref[k : k + step, :] += jnp.dot(
            dscores, query_ref[...], preferred_element_type=F32
        )
        query_term = query_term + contract_first(dscores, key_ref[k : k + step, :])
    query_term_ref[...] = query_term


def attend_back_scores(prob, weight, values, datt, delta, queries, keys_x):
    keys, count = prob.shape
    head = values.shape[1]
    tile = count // 4
    across = pl.BlockSpec((tile, head), lambda j: (j, 0))
    down = pl.BlockSpec((keys, head), lambda j: (0, 0))
    return pl.pallas_call(
        back_scores_kernel,
        grid=(4,),
        in_specs=[
            pl.BlockSpec((keys, tile), lambda j: (0, j)),
            pl.BlockSpec((1, tile), lambda j: (0, j)),
            down,
            across,
            pl.BlockSpec((1, tile), lambda j: (0, j)),
            across,
            down,
        ],
        out_specs=[down, across],
        out_shape=[
            jax.ShapeDtypeStruct((keys, head), F32),
            jax.ShapeDtypeStruct((count, head), F32),
        ],
        cost_estimate=pl.CostEstimate(
            flops=6 * keys * count * head, bytes_accessed=2 * keys * count, transcendentals=0
        ),
        compiler_params=pltpu.CompilerParams(vmem_limit_bytes=32 * 1024 * 1024),
    )(prob, weight, values, datt, delta, queries, keys_x)


def terms_kernel(left_ref, right_ref, mine_ref, theirs_ref):
    n_y, n_z, piece, half = mine_ref.shape[1:]
    panel = n_y * piece
    for z in range(n_z):
        out = contract_first(left_ref[:, z * panel : (z + 1) * panel], right_ref[...])
        out = out.astype(BF16).reshape(n_y, piece, 2 * half)
        mine_ref[0, :, z] = out[:, :, :half]
        theirs_ref[0, :, z] = out[:, :, half:]


def panel_terms(left, right, n_x, n_y, n_z):
    rows, width = left.shape
    half = right.shape[1] // 2
    piece = width // (n_x * n_y * n_z)
    block = (1, n_y, n_z, piece, half)
    spec = pl.BlockSpec(block, lambda x: (x, 0, 0, 0, 0))
    shape = jax.ShapeDtypeStruct((n_x,) + block[1:], BF16)
    return pl.pallas_call(
        terms_kernel,
        grid=(n_x,),
        in_specs=[
            pl.BlockSpec((rows, width // n_x), lambda x: (0, x)),
            pl.BlockSpec(right.shape, lambda x: (0, 0)),
        ],
        out_specs=[spec, spec],
        out_shape=[shape, shape],
        cost_estimate=pl.CostEstimate(
            flops=4 * rows * width * half,
            bytes_accessed=2 * rows * width + 4 * width * half,
            transcendentals=0,
        ),
        compiler_params=pltpu.CompilerParams(vmem_limit_bytes=32 * 1024 * 1024),
    )(left, right)


def sum_plane_kernel(n_zl, n_zh, got_ref, out_ref):
    members, _, half = got_ref.shape
    small = out_ref.shape[1] // 2
    n_value = n_zl * n_zh * 2 * small
    n_y = 2 * n_zl
    part = small // 2
    total = F32(0.0)
    for m in range(members):
        total = total + got_ref[m, :n_value, :].astype(F32)
    total = total.astype(BF16)
    for zh in range(n_zh):
        for c in range(2):
            for zl in range(n_zl):
                row = ((zh * 2 + c) * n_zl + zl) * small
                out_ref[zl * n_zh + zh, c * small : (c + 1) * small, :half] = total[
                    row : row + small
                ]
    for zl in range(n_zl):
        sums = []
        for y in (2 * zl, 2 * zl + 1):
            total = F32(0.0)
            for x in range(members // n_y):
                total = total + got_ref[x * n_y + y, n_value:, :].astype(F32)
            sums.append(total)
        for zh in range(n_zh):
            for c in range(2):
                row = (zh * 2 + c) * part
                both = jnp.concatenate([t[row : row + part] for t in sums], axis=0)
                out_ref[zl * n_zh + zh, c * small : (c + 1) * small, half:] = both.astype(BF16)


def sum_plane(got, n_x, n_zl, n_zh):
    members, rows, half = got.shape
    small = rows * 4 // 5 // (n_zl * n_zh * 2)
    return pl.pallas_call(
        functools.partial(sum_plane_kernel, n_zl, n_zh),
        out_shape=jax.ShapeDtypeStruct((n_zl * n_zh, 2 * small, 2 * half), BF16),
        compiler_params=pltpu.CompilerParams(vmem_limit_bytes=32 * 1024 * 1024),
    )(got)


def place_rows_kernel(n_zl, n_y, got_ref, value_ref, output_ref):
    small = got_ref.shape[1]
    half = got_ref.shape[2] // 2
    part = small // 2
    for zl in range(n_zl):
        for y in range(n_y):
            for c in range(2):
                got = got_ref[(zl * n_y + y) * 2 + c].astype(F32)
                columns = slice(c * half, (c + 1) * half)
                row = (y * n_zl + zl) * small
                value_ref[row : row + small, columns] = got[:, :half]
                for k in range(2):
                    row = ((zl * 2 + k) * n_y + y) * part
                    output_ref[row : row + part, columns] = got[k * part : (k + 1) * part, half:]


def place_rows(got, n_zl, n_y):
    _, small, width = got.shape
    shape = jax.ShapeDtypeStruct((n_zl * n_y * small, width), F32)
    return pl.pallas_call(
        functools.partial(place_rows_kernel, n_zl, n_y), out_shape=[shape, shape]
    )(got)


def body(
    tokens,
    queries,
    key_vectors,
    doc_position,
    value_scores,
    value_experts,
    output_scores,
    output_experts,
    value_panels,
    output_panels,
    cotangent,
):
    n_x, n_y, n_zh, n_zl = 4, 4, 4, 2
    tok_block = tokens[0]
    query_block = queries[0]
    own_keys = key_vectors[0]
    positions = doc_position[0]
    grad_rows = cotangent[0]
    rows, width = tok_block.shape
    head = query_block.shape[1]
    experts = value_scores.shape[2]
    panel_rows, panel_width = value_panels.shape
    half = panel_width // 2
    ix, iy = lax.axis_index("x"), lax.axis_index("y")
    izh, ic = lax.axis_index("zh"), lax.axis_index("c")
    first = ic == 0

    def own_first(pair):
        return jnp.where(first, pair, pair[::-1])

    def gate_own_first(gate):
        return own_first(gate.T.reshape(2, experts // 2, rows)).reshape(experts, rows).T

    starts = (ic * half, (1 - ic) * half)
    mine, theirs = (
        jnp.concatenate(
            [lax.dynamic_slice_in_dim(p, at, half, 1) for p in (value_panels, output_panels)],
            axis=1,
        )
        for at in starts
    )
    pair = own_first(jnp.stack([mine, other_core(theirs)])).reshape(2 * panel_rows, 2 * half)
    quarter = 2 * panel_rows // n_y
    pair = lax.dynamic_slice_in_dim(pair, iy * quarter, quarter, 0)

    def fold(vecs):
        return jnp.concatenate([vecs[: rows // 2], vecs[rows // 2 :]], axis=1)

    def unfold(packed):
        return jnp.concatenate([packed[:, :, :head], packed[:, :, head:]], axis=1)

    pos_hi = (positions // 128).astype(BF16)
    pos_lo = (positions % 128).astype(BF16)
    pos_rows = jnp.zeros((16, half), BF16)
    pos_rows = pos_rows.at[0, :rows].set(pos_hi).at[1, :rows].set(pos_lo)
    packed = jnp.concatenate(
        [pair[:, :half], pair[:, half:], fold(query_block), pos_rows], axis=0
    )
    packed = share(packed, "zh", n_zh)
    packed, vs, ve, os, oe = lax.optimization_barrier(
        (packed, value_scores[0], value_experts[0], output_scores[0], output_experts[0])
    )
    value_gate = gate_own_first(expert_gates(vs, ve, experts))
    output_gate = gate_own_first(expert_gates(os, oe, experts))
    value_zh = ring_share(packed[:, :quarter], "y", n_y, 1).reshape(n_zh * n_y * quarter, half)
    packed = packed[:, quarter:]
    output_zh = packed[:, :quarter].reshape(n_zh * quarter, half)
    queries_zh = unfold(packed[:, quarter : quarter + rows // 2]).reshape(n_zh * rows, head)
    pos_zh = packed[:, quarter + rows // 2 : quarter + rows // 2 + 2, :rows]
    packed = share(jnp.concatenate([output_zh, fold(own_keys)], axis=0), "x", n_x)
    output_x = packed[:, : n_zh * quarter].reshape(n_x, n_zh, quarter, half)
    keys_x = unfold(packed[:, n_zh * quarter :]).reshape(n_x * rows, head)
    value_parts = [value_zh] * n_x
    for step in (1, 3):
        value_parts[step] = lax.ppermute(value_zh, "x", shifted(n_x, step))
    value_parts[1:] = lax.optimization_barrier(value_parts[1:])
    value_parts[2] = lax.ppermute(value_parts[2], "x", shifted(n_x, 2))
    output_parts = shifted_blocks(output_x, "y", n_y)
    queries_all = jnp.concatenate([queries_zh, other_core(queries_zh)], axis=0)
    pos_pair = jnp.stack([pos_zh, other_core(pos_zh)]).astype(F32)
    pos_all = (pos_pair[:, :, 0] * 128.0 + pos_pair[:, :, 1]).astype(jnp.int32).reshape(-1)

    count = queries_all.shape[0]
    scale = head ** (-0.5)
    core_of = own_first(jnp.arange(2, dtype=jnp.int32))
    query_index = (
        ((ix * n_zh + jnp.arange(n_zh, dtype=jnp.int32))[None, :, None] * 2 + core_of[:, None, None])
        * rows
        + jnp.arange(rows, dtype=jnp.int32)[None, None, :]
    ).reshape(-1)
    key_index = (
        ((jnp.arange(n_x, dtype=jnp.int32) * n_zh + izh) * 2 + ic)[:, None] * rows
        + jnp.arange(rows, dtype=jnp.int32)[None, :]
    ).reshape(-1)
    visible = (key_index[:, None] <= query_index[None, :]) & (
        key_index[:, None] >= (query_index - pos_all)[None, :]
    )
    masked = jnp.where(visible, contract_last(keys_x, queries_all) * scale, -jnp.inf)
    top = jnp.maximum(jnp.max(masked, axis=0), -1e30)
    total = jnp.sum(jnp.exp(masked - top[None, :]), axis=0)
    prob_low = jnp.exp(masked - top[None, :]).astype(BF16)
    top, total, prob_low, value_parts, output_parts = lax.optimization_barrier(
        (top, total, prob_low, value_parts, output_parts)
    )
    stats = jnp.stack([top, total]).reshape(2, 2, count // 2)
    stats = jnp.where(first, stats, stats[:, ::-1])
    stats = share(stats, ("zh", "c"), n_zh * 2)
    value_mine = in_order(value_parts, "x", 0).reshape(width, half)
    value_own = jnp.concatenate([value_mine, other_core(value_mine)], axis=1)
    output_mine = in_order(output_parts, "y", 2).reshape(width, half)
    output_own = jnp.concatenate([output_mine, other_core(output_mine)], axis=1)

    projection = jnp.dot(tok_block, value_own, preferred_element_type=F32)
    value_vec = gather_experts(value_gate, projection)
    values_x = ring_share(value_vec, "x", n_x, 0).reshape(n_x * rows, head)

    pulled = jnp.dot(grad_rows, output_own, preferred_element_type=F32)
    dattended = gather_experts(output_gate, pulled)
    stats, _, _ = lax.optimization_barrier((stats, value_vec, dattended))
    all_top = jnp.max(stats[:, 0], axis=0)
    all_total = jnp.sum(stats[:, 1] * jnp.exp(stats[:, 0] - all_top[None]), axis=0)
    log_total = own_first(all_top + jnp.log(all_total)).reshape(-1)
    weight = jnp.exp(top - log_total)
    datt_zh = ring_share(dattended, "zh", n_zh, 0).reshape(n_zh * rows, head)
    datt_all = jnp.concatenate([datt_zh, other_core(datt_zh)], axis=0)

    def sum_queries(term):
        return term[: count // 2] + other_core(term[count // 2 :].astype(BF16)).astype(F32)

    attended = contract_first(prob_low, values_x) * weight[:, None]
    attended = sum_queries(attended).astype(BF16)
    attended, datt_all = lax.optimization_barrier((attended, datt_all))
    attended = sum_bf16(list(exchange(attended.reshape(n_zh, rows, head), "zh")))

    weight = weight.reshape(1, count)
    delta, value_term = attend_back_values(prob_low, weight, values_x, datt_all)
    delta, attended = lax.optimization_barrier((delta.reshape(2, count // 2), attended))
    delta = share(own_first(delta), ("zh", "c"), n_zh * 2)
    row_delta = own_first(jnp.sum(delta, axis=0)).reshape(1, count)
    expanded = expand(output_gate, attended)

    mine, theirs = panel_terms(grad_rows, expanded, n_x, n_y, n_zh * 2)
    row_delta, theirs = lax.optimization_barrier((row_delta, theirs))
    chip_output = add_bf16(mine, other_core(theirs))
    key_term, query_term = attend_back_scores(
        prob_low, weight, values_x, datt_all, row_delta, queries_all, keys_x
    )

    key_value = jnp.concatenate([(key_term * scale).astype(BF16), value_term.astype(BF16)], axis=1)
    key_value, chip_output = lax.optimization_barrier((key_value, chip_output))
    parts = ring_parts(chip_output.transpose(1, 0, 2, 3, 4), "y", n_y, ordered=True)
    key_value = exchange(key_value.reshape(n_x, rows, 2 * head), "x")
    key_value = jnp.sum(key_value.astype(F32), axis=0).astype(BF16)
    grad_keys = key_value[:, :head]
    dvalue = key_value[:, head:]
    dvalue, parts[1], parts[3] = lax.optimization_barrier((dvalue, parts[1], parts[3]))
    value_grad = expand(value_gate, dvalue)

    mine, theirs = panel_terms(tok_block, value_grad, n_x, n_y, n_zh * 2)
    piece = panel_rows // n_y
    part = piece // n_y
    chip_value = add_bf16(mine, other_core(theirs))
    chip_value, query_term, value_grad, expanded, parts[2] = lax.optimization_barrier(
        (chip_value, query_term, value_grad, expanded, parts[2])
    )
    chip_output = sum_bf16(parts)
    chip_value = chip_value.reshape(n_x * n_y, n_zh * 2 * piece, half)
    chip_output = chip_output.reshape(n_x, n_zh * 2, n_y, part, half).transpose(0, 2, 1, 3, 4)
    chip_output = chip_output.reshape(n_x * n_y, n_zh * 2 * part, half)
    plane = exchange(jnp.concatenate([chip_value, chip_output], axis=1), ("x", "y"))

    grad_queries = sum_queries(query_term * scale).astype(BF16)
    grad_queries = ring_sum(grad_queries.reshape(n_zh, rows, head), "zh", n_zh)
    layer_output = contract_last(expanded, output_own).astype(BF16)
    grad_tokens = contract_last(value_grad, value_own).astype(BF16)
    plane, layer_output, grad_tokens, grad_queries = lax.optimization_barrier(
        (plane, layer_output, grad_tokens, grad_queries)
    )
    small = piece // n_zl
    plane = sum_plane(plane, n_x, n_zl, n_zh)
    plane = exchange(plane, ("zl", "zh"))
    whole = jnp.sum(plane.astype(F32), axis=0).astype(BF16).reshape(2, small, panel_width)
    whole = jnp.broadcast_to(whole[None], (n_zl * n_y,) + whole.shape)
    whole = exchange(whole.reshape(n_zl * n_y * 2, small, panel_width), ("zl", "y", "c"))
    grad_value, grad_output = place_rows(whole, n_zl, n_y)
    return (
        layer_output[None],
        grad_tokens[None],
        grad_queries[None],
        grad_keys[None],
        grad_value,
        grad_output,
    )


def solution(mesh):
    chips = Mesh(mesh.devices.reshape(2, 4, 4, 4, 2), ("zl", "y", "x", "zh", "c"))
    batch, place = ("zl", "y"), ("x", "zh", "c")
    wide = P(batch, place, None)
    panel = P(place, None)
    in_specs = (wide, wide, wide, P(batch, place), wide, wide, wide, wide, panel, panel, wide)
    out_specs = (wide, wide, wide, wide, panel, panel)
    return jax.shard_map(
        body, mesh=chips, in_specs=in_specs, out_specs=out_specs, check_vma=False
    )
```

```python
import functools

import jax
import jax.numpy as jnp
from jax import lax
from jax.experimental import pallas as pl
from jax.experimental.pallas import tpu as pltpu
from jax.sharding import Mesh, PartitionSpec as P

F32 = jnp.float32
BF16 = jnp.bfloat16


def expert_gates(scores, chosen, experts):
    chosen_hit = chosen[:, :, None] == lax.iota(jnp.int32, experts)[None, None, :]
    return jnp.where(jnp.any(chosen_hit, axis=1), scores, F32(0.0))


def contract_last(left, right):
    return lax.dot_general(left, right, (((1,), (1,)), ((), ())), preferred_element_type=F32)


def contract_first(left, right):
    return lax.dot_general(left, right, (((0,), (0,)), ((), ())), preferred_element_type=F32)


def exchange(blocks, axes):
    return lax.all_to_all(blocks, axes, 0, 0, tiled=True)


def share(block, axes, count):
    return exchange(jnp.broadcast_to(block[None], (count,) + block.shape), axes)


def gather_experts(gate, panels):
    head = panels.shape[1] // gate.shape[1]
    total = F32(0.0)
    for e in range(gate.shape[1]):
        total = total + panels[:, e * head : (e + 1) * head] * gate[:, e : e + 1]
    return total.astype(BF16)


def expand(gate, vec):
    vec = vec.astype(F32)
    return jnp.concatenate(
        [(gate[:, e : e + 1] * vec).astype(BF16) for e in range(gate.shape[1])], axis=1
    )


def other_core(value):
    return lax.ppermute(value, "c", [(0, 1), (1, 0)])


def shifted(count, step):
    return [(k, (k + step) % count) for k in range(count)]


def ring_share(block, axis, count, at):
    place = lax.axis_index(axis)
    return in_order(shifted_blocks(block, axis, count), axis, at)


def shifted_blocks(block, axis, count):
    return [block] + [lax.ppermute(block, axis, shifted(count, k)) for k in range(1, count)]


def in_order(parts, axis, at):
    place, count = lax.axis_index(axis), len(parts)
    ordered = [lax.select_n((place - member) % count, *parts) for member in range(count)]
    return jnp.stack(ordered, axis=at)


def ring_parts(blocks, axis, count, ordered=False):
    place = lax.axis_index(axis)
    parts = [
        lax.dynamic_index_in_dim(blocks, (place + step) % count, 0, keepdims=False)
        for step in range(count)
    ]
    for step in (1, 3):
        parts[step] = lax.ppermute(parts[step], axis, shifted(count, step))
    if ordered:
        parts[1], parts[2], parts[3] = lax.optimization_barrier((parts[1], parts[2], parts[3]))
    parts[2] = lax.ppermute(parts[2], axis, shifted(count, 2))
    return parts


def sum_bf16(parts):
    return sum(part.astype(F32) for part in parts).astype(BF16)


def ring_sum(blocks, axis, count):
    return sum_bf16(ring_parts(blocks, axis, count))


def add_bf16(left, right):
    return (left.astype(F32) + right.astype(F32)).astype(BF16)


def back_values_kernel(prob_ref, weight_ref, value_ref, datt_ref, delta_ref, term_ref):
    @pl.when(pl.program_id(0) == 0)
    def _():
        term_ref[...] = jnp.zeros_like(term_ref)

    keys = prob_ref.shape[0]
    step = keys // 4
    delta = F32(0.0)
    for k in range(0, keys, step):
        prob = prob_ref[k : k + step, :].astype(F32) * weight_ref[...]
        dweights = contract_last(value_ref[k : k + step, :], datt_ref[...])
        delta = delta + jnp.sum(prob * dweights, axis=0, keepdims=True)
        term_ref[k : k + step, :] += jnp.dot(
            prob.astype(BF16), datt_ref[...], preferred_element_type=F32
        )
    delta_ref[...] = delta


def attend_back_values(prob, weight, values, datt):
    keys, count = prob.shape
    head = values.shape[1]
    tile = count // 4
    return pl.pallas_call(
        back_values_kernel,
        grid=(4,),
        in_specs=[
            pl.BlockSpec((keys, tile), lambda j: (0, j)),
            pl.BlockSpec((1, tile), lambda j: (0, j)),
            pl.BlockSpec((keys, head), lambda j: (0, 0)),
            pl.BlockSpec((tile, head), lambda j: (j, 0)),
        ],
        out_specs=[
            pl.BlockSpec((1, tile), lambda j: (0, j)),
            pl.BlockSpec((keys, head), lambda j: (0, 0)),
        ],
        out_shape=[
            jax.ShapeDtypeStruct((1, count), F32),
            jax.ShapeDtypeStruct((keys, head), F32),
        ],
        cost_estimate=pl.CostEstimate(
            flops=4 * keys * count * head, bytes_accessed=2 * keys * count, transcendentals=0
        ),
        compiler_params=pltpu.CompilerParams(vmem_limit_bytes=32 * 1024 * 1024),
    )(prob, weight, values, datt)


def back_scores_kernel(
    prob_ref,
    weight_ref,
    value_ref,
    datt_ref,
    delta_ref,
    query_ref,
    key_ref,
    key_term_ref,
    query_term_ref,
):
    @pl.when(pl.program_id(0) == 0)
    def _():
        key_term_ref[...] = jnp.zeros_like(key_term_ref)

    keys = prob_ref.shape[0]
    step = keys // 4
    query_term = F32(0.0)
    for k in range(0, keys, step):
        dweights = contract_last(value_ref[k : k + step, :], datt_ref[...])
        prob = prob_ref[k : k + step, :].astype(F32) * weight_ref[...]
        dscores = (prob * (dweights - delta_ref[...])).astype(BF16)
        key_term_ref[k : k + step, :] += jnp.dot(
            dscores, query_ref[...], preferred_element_type=F32
        )
        query_term = query_term + contract_first(dscores, key_ref[k : k + step, :])
    query_term_ref[...] = query_term


def attend_back_scores(prob, weight, values, datt, delta, queries, keys_x):
    keys, count = prob.shape
    head = values.shape[1]
    tile = count // 4
    across = pl.BlockSpec((tile, head), lambda j: (j, 0))
    down = pl.BlockSpec((keys, head), lambda j: (0, 0))
    return pl.pallas_call(
        back_scores_kernel,
        grid=(4,),
        in_specs=[
            pl.BlockSpec((keys, tile), lambda j: (0, j)),
            pl.BlockSpec((1, tile), lambda j: (0, j)),
            down,
            across,
            pl.BlockSpec((1, tile), lambda j: (0, j)),
            across,
            down,
        ],
        out_specs=[down, across],
        out_shape=[
            jax.ShapeDtypeStruct((keys, head), F32),
            jax.ShapeDtypeStruct((count, head), F32),
        ],
        cost_estimate=pl.CostEstimate(
            flops=6 * keys * count * head, bytes_accessed=2 * keys * count, transcendentals=0
        ),
        compiler_params=pltpu.CompilerParams(vmem_limit_bytes=32 * 1024 * 1024),
    )(prob, weight, values, datt, delta, queries, keys_x)


def terms_kernel(left_ref, right_ref, mine_ref, theirs_ref):
    n_y, n_z, piece, half = mine_ref.shape[1:]
    panel = n_y * piece
    for z in range(n_z):
        out = contract_first(left_ref[:, z * panel : (z + 1) * panel], right_ref[...])
        out = out.astype(BF16).reshape(n_y, piece, 2 * half)
        mine_ref[0, :, z] = out[:, :, :half]
        theirs_ref[0, :, z] = out[:, :, half:]


def panel_terms(left, right, n_x, n_y, n_z):
    rows, width = left.shape
    half = right.shape[1] // 2
    piece = width // (n_x * n_y * n_z)
    block = (1, n_y, n_z, piece, half)
    spec = pl.BlockSpec(block, lambda x: (x, 0, 0, 0, 0))
    shape = jax.ShapeDtypeStruct((n_x,) + block[1:], BF16)
    return pl.pallas_call(
        terms_kernel,
        grid=(n_x,),
        in_specs=[
            pl.BlockSpec((rows, width // n_x), lambda x: (0, x)),
            pl.BlockSpec(right.shape, lambda x: (0, 0)),
        ],
        out_specs=[spec, spec],
        out_shape=[shape, shape],
        cost_estimate=pl.CostEstimate(
            flops=4 * rows * width * half,
            bytes_accessed=2 * rows * width + 4 * width * half,
            transcendentals=0,
        ),
        compiler_params=pltpu.CompilerParams(vmem_limit_bytes=32 * 1024 * 1024),
    )(left, right)


def sum_plane_kernel(n_zl, n_zh, got_ref, out_ref):
    members, _, half = got_ref.shape
    small = out_ref.shape[1] // 2
    n_value = n_zl * n_zh * 2 * small
    n_y = 2 * n_zl
    part = small // 2
    total = F32(0.0)
    for m in range(members):
        total = total + got_ref[m, :n_value, :].astype(F32)
    total = total.astype(BF16)
    for zh in range(n_zh):
        for c in range(2):
            for zl in range(n_zl):
                row = ((zh * 2 + c) * n_zl + zl) * small
                out_ref[zl * n_zh + zh, c * small : (c + 1) * small, :half] = total[
                    row : row + small
                ]
    for zl in range(n_zl):
        sums = []
        for y in (2 * zl, 2 * zl + 1):
            total = F32(0.0)
            for x in range(members // n_y):
                total = total + got_ref[x * n_y + y, n_value:, :].astype(F32)
            sums.append(total)
        for zh in range(n_zh):
            for c in range(2):
                row = (zh * 2 + c) * part
                both = jnp.concatenate([t[row : row + part] for t in sums], axis=0)
                out_ref[zl * n_zh + zh, c * small : (c + 1) * small, half:] = both.astype(BF16)


def sum_plane(got, n_x, n_zl, n_zh):
    members, rows, half = got.shape
    small = rows * 4 // 5 // (n_zl * n_zh * 2)
    return pl.pallas_call(
        functools.partial(sum_plane_kernel, n_zl, n_zh),
        out_shape=jax.ShapeDtypeStruct((n_zl * n_zh, 2 * small, 2 * half), BF16),
        compiler_params=pltpu.CompilerParams(vmem_limit_bytes=32 * 1024 * 1024),
    )(got)


def place_rows_kernel(n_zl, n_y, got_ref, value_ref, output_ref):
    small = got_ref.shape[1]
    half = got_ref.shape[2] // 2
    part = small // 2
    for zl in range(n_zl):
        for y in range(n_y):
            for c in range(2):
                got = got_ref[(zl * n_y + y) * 2 + c].astype(F32)
                columns = slice(c * half, (c + 1) * half)
                row = (y * n_zl + zl) * small
                value_ref[row : row + small, columns] = got[:, :half]
                for k in range(2):
                    row = ((zl * 2 + k) * n_y + y) * part
                    output_ref[row : row + part, columns] = got[k * part : (k + 1) * part, half:]


def place_rows(got, n_zl, n_y):
    _, small, width = got.shape
    shape = jax.ShapeDtypeStruct((n_zl * n_y * small, width), F32)
    return pl.pallas_call(
        functools.partial(place_rows_kernel, n_zl, n_y), out_shape=[shape, shape]
    )(got)


def body(
    tokens,
    queries,
    key_vectors,
    doc_position,
    value_scores,
    value_experts,
    output_scores,
    output_experts,
    value_panels,
    output_panels,
    cotangent,
):
    n_x, n_y, n_zh, n_zl = 4, 4, 4, 2
    tok_block = tokens[0]
    query_block = queries[0]
    own_keys = key_vectors[0]
    positions = doc_position[0]
    grad_rows = cotangent[0]
    rows, width = tok_block.shape
    head = query_block.shape[1]
    experts = value_scores.shape[2]
    panel_rows, panel_width = value_panels.shape
    half = panel_width // 2
    ix, iy = lax.axis_index("x"), lax.axis_index("y")
    izh, ic = lax.axis_index("zh"), lax.axis_index("c")
    first = ic == 0

    def own_first(pair):
        return jnp.where(first, pair, pair[::-1])

    def gate_own_first(gate):
        return own_first(gate.T.reshape(2, experts // 2, rows)).reshape(experts, rows).T

    starts = (ic * half, (1 - ic) * half)
    mine, theirs = (
        jnp.concatenate(
            [lax.dynamic_slice_in_dim(p, at, half, 1) for p in (value_panels, output_panels)],
            axis=1,
        )
        for at in starts
    )
    pair = own_first(jnp.stack([mine, other_core(theirs)])).reshape(2 * panel_rows, 2 * half)
    quarter = 2 * panel_rows // n_y
    pair = lax.dynamic_slice_in_dim(pair, iy * quarter, quarter, 0)

    def fold(vecs):
        return jnp.concatenate([vecs[: rows // 2], vecs[rows // 2 :]], axis=1)

    def unfold(packed):
        return jnp.concatenate([packed[:, :, :head], packed[:, :, head:]], axis=1)

    pos_hi = (positions // 128).astype(BF16)
    pos_lo = (positions % 128).astype(BF16)
    pos_rows = jnp.zeros((16, half), BF16)
    pos_rows = pos_rows.at[0, :rows].set(pos_hi).at[1, :rows].set(pos_lo)
    packed = jnp.concatenate(
        [pair[:, :half], pair[:, half:], fold(query_block), pos_rows], axis=0
    )
    packed = share(packed, "zh", n_zh)
    packed, vs, ve, os, oe = lax.optimization_barrier(
        (packed, value_scores[0], value_experts[0], output_scores[0], output_experts[0])
    )
    value_gate = gate_own_first(expert_gates(vs, ve, experts))
    output_gate = gate_own_first(expert_gates(os, oe, experts))
    value_zh = ring_share(packed[:, :quarter], "y", n_y, 1).reshape(n_zh * n_y * quarter, half)
    packed = packed[:, quarter:]
    output_zh = packed[:, :quarter].reshape(n_zh * quarter, half)
    queries_zh = unfold(packed[:, quarter : quarter + rows // 2]).reshape(n_zh * rows, head)
    pos_zh = packed[:, quarter + rows // 2 : quarter + rows // 2 + 2, :rows]
    packed = share(jnp.concatenate([output_zh, fold(own_keys)], axis=0), "x", n_x)
    output_x = packed[:, : n_zh * quarter].reshape(n_x, n_zh, quarter, half)
    keys_x = unfold(packed[:, n_zh * quarter :]).reshape(n_x * rows, head)
    value_parts = [value_zh] * n_x
    for step in (1, 3):
        value_parts[step] = lax.ppermute(value_zh, "x", shifted(n_x, step))
    value_parts[1:] = lax.optimization_barrier(value_parts[1:])
    value_parts[2] = lax.ppermute(value_parts[2], "x", shifted(n_x, 2))
    output_parts = shifted_blocks(output_x, "y", n_y)
    queries_all = jnp.concatenate([queries_zh, other_core(queries_zh)], axis=0)
    pos_pair = jnp.stack([pos_zh, other_core(pos_zh)]).astype(F32)
    pos_all = (pos_pair[:, :, 0] * 128.0 + pos_pair[:, :, 1]).astype(jnp.int32).reshape(-1)

    count = queries_all.shape[0]
    scale = head ** (-0.5)
    core_of = own_first(jnp.arange(2, dtype=jnp.int32))
    query_index = (
        ((ix * n_zh + jnp.arange(n_zh, dtype=jnp.int32))[None, :, None] * 2 + core_of[:, None, None])
        * rows
        + jnp.arange(rows, dtype=jnp.int32)[None, None, :]
    ).reshape(-1)
    key_index = (
        ((jnp.arange(n_x, dtype=jnp.int32) * n_zh + izh) * 2 + ic)[:, None] * rows
        + jnp.arange(rows, dtype=jnp.int32)[None, :]
    ).reshape(-1)
    visible = (key_index[:, None] <= query_index[None, :]) & (
        key_index[:, None] >= (query_index - pos_all)[None, :]
    )
    masked = jnp.where(visible, contract_last(keys_x, queries_all) * scale, -jnp.inf)
    top = jnp.maximum(jnp.max(masked, axis=0), -1e30)
    total = jnp.sum(jnp.exp(masked - top[None, :]), axis=0)
    prob_low = jnp.exp(masked - top[None, :]).astype(BF16)
    top, total, prob_low, value_parts, output_parts = lax.optimization_barrier(
        (top, total, prob_low, value_parts, output_parts)
    )
    stats = jnp.stack([top, total]).reshape(2, 2, count // 2)
    stats = jnp.where(first, stats, stats[:, ::-1])
    stats = share(stats, ("zh", "c"), n_zh * 2)
    value_mine = in_order(value_parts, "x", 0).reshape(width, half)
    value_own = jnp.concatenate([value_mine, other_core(value_mine)], axis=1)
    output_mine = in_order(output_parts, "y", 2).reshape(width, half)
    output_own = jnp.concatenate([output_mine, other_core(output_mine)], axis=1)

    projection = jnp.dot(tok_block, value_own, preferred_element_type=F32)
    value_vec = gather_experts(value_gate, projection)
    values_x = ring_share(value_vec, "x", n_x, 0).reshape(n_x * rows, head)

    pulled = jnp.dot(grad_rows, output_own, preferred_element_type=F32)
    dattended = gather_experts(output_gate, pulled)
    stats, _, _ = lax.optimization_barrier((stats, value_vec, dattended))
    all_top = jnp.max(stats[:, 0], axis=0)
    all_total = jnp.sum(stats[:, 1] * jnp.exp(stats[:, 0] - all_top[None]), axis=0)
    log_total = own_first(all_top + jnp.log(all_total)).reshape(-1)
    weight = jnp.exp(top - log_total)
    datt_zh = ring_share(dattended, "zh", n_zh, 0).reshape(n_zh * rows, head)
    datt_all = jnp.concatenate([datt_zh, other_core(datt_zh)], axis=0)

    def sum_queries(term):
        return term[: count // 2] + other_core(term[count // 2 :].astype(BF16)).astype(F32)

    attended = contract_first(prob_low, values_x) * weight[:, None]
    attended = sum_queries(attended).astype(BF16)
    attended, datt_all = lax.optimization_barrier((attended, datt_all))
    attended = sum_bf16(list(exchange(attended.reshape(n_zh, rows, head), "zh")))

    weight = weight.reshape(1, count)
    delta, value_term = attend_back_values(prob_low, weight, values_x, datt_all)
    delta, attended = lax.optimization_barrier((delta.reshape(2, count // 2), attended))
    delta = share(own_first(delta), ("zh", "c"), n_zh * 2)
    row_delta = own_first(jnp.sum(delta, axis=0)).reshape(1, count)
    expanded = expand(output_gate, attended)

    mine, theirs = panel_terms(grad_rows, expanded, n_x, n_y, n_zh * 2)
    chip_output = add_bf16(mine, other_core(theirs))
    row_delta, chip_output = lax.optimization_barrier((row_delta, chip_output))
    key_term, query_term = attend_back_scores(
        prob_low, weight, values_x, datt_all, row_delta, queries_all, keys_x
    )

    key_value = jnp.concatenate([(key_term * scale).astype(BF16), value_term.astype(BF16)], axis=1)
    parts = ring_parts(chip_output.transpose(1, 0, 2, 3, 4), "y", n_y, ordered=True)
    key_value, parts[1], parts[3] = lax.optimization_barrier((key_value, parts[1], parts[3]))
    key_value = exchange(key_value.reshape(n_x, rows, 2 * head), "x")
    key_value = jnp.sum(key_value.astype(F32), axis=0).astype(BF16)
    grad_keys = key_value[:, :head]
    dvalue = key_value[:, head:]
    dvalue, parts[2] = lax.optimization_barrier((dvalue, parts[2]))
    chip_output = sum_bf16(parts)
    value_grad = expand(value_gate, dvalue)

    mine, theirs = panel_terms(tok_block, value_grad, n_x, n_y, n_zh * 2)
    piece = panel_rows // n_y
    part = piece // n_y
    chip_value = add_bf16(mine, other_core(theirs))
    chip_value, query_term, value_grad, expanded = lax.optimization_barrier(
        (chip_value, query_term, value_grad, expanded)
    )
    chip_value = chip_value.reshape(n_x * n_y, n_zh * 2 * piece, half)
    chip_output = chip_output.reshape(n_x, n_zh * 2, n_y, part, half).transpose(0, 2, 1, 3, 4)
    chip_output = chip_output.reshape(n_x * n_y, n_zh * 2 * part, half)
    plane = exchange(jnp.concatenate([chip_value, chip_output], axis=1), ("x", "y"))

    grad_queries = sum_queries(query_term * scale).astype(BF16)
    grad_queries = ring_sum(grad_queries.reshape(n_zh, rows, head), "zh", n_zh)
    layer_output = contract_last(expanded, output_own).astype(BF16)
    grad_tokens = contract_last(value_grad, value_own).astype(BF16)
    plane, layer_output, grad_tokens, grad_queries = lax.optimization_barrier(
        (plane, layer_output, grad_tokens, grad_queries)
    )
    small = piece // n_zl
    plane = sum_plane(plane, n_x, n_zl, n_zh)
    plane = exchange(plane, ("zl", "zh"))
    whole = jnp.sum(plane.astype(F32), axis=0).astype(BF16).reshape(2, small, panel_width)
    whole = jnp.broadcast_to(whole[None], (n_zl * n_y,) + whole.shape)
    whole = exchange(whole.reshape(n_zl * n_y * 2, small, panel_width), ("zl", "y", "c"))
    grad_value, grad_output = place_rows(whole, n_zl, n_y)
    return (
        layer_output[None],
        grad_tokens[None],
        grad_queries[None],
        grad_keys[None],
        grad_value,
        grad_output,
    )


def solution(mesh):
    chips = Mesh(mesh.devices.reshape(2, 4, 4, 4, 2), ("zl", "y", "x", "zh", "c"))
    batch, place = ("zl", "y"), ("x", "zh", "c")
    wide = P(batch, place, None)
    panel = P(place, None)
    in_specs = (wide, wide, wide, P(batch, place), wide, wide, wide, wide, panel, panel, wide)
    out_specs = (wide, wide, wide, wide, panel, panel)
    return jax.shard_map(
        body, mesh=chips, in_specs=in_specs, out_specs=out_specs, check_vma=False
    )
```
